512 devices in a mesh: af: 8 (over x, z_hi), vert: 64 (over y, z_lo, core).
Axes of the slice: x: 4, y: 4, z: 16 (z_hi: 2, z_lo: 8; z = z_hi * 8 + z_lo), core: 2. Of those that a mesh axis runs over, the one named last changes fastest.
Arguments:
- signals: bfloat16 [1000, 16384], P('af', 'vert'), may hold values from -2000 to 2000
- basis: bfloat16 [10, 1000], P(None, 'af'), may hold values from -0.1875 to 0.1875
- atoms: float32 [10, 262144], P(None, ('af', 'vert')), may hold values from -6 to 6
- params: float32 [3, 262144], P(None, ('af', 'vert')), may hold values from -1.5 to 1.5
Outputs:
- coefficients: float32 [10, 16384], P(None, 'vert')
- maps: float32 [3, 16384], P(None, 'vert')
The draws below stay inside these ranges and needn't reach their ends.
All inputs are finite; a program needn't handle non-finite values.
Results may differ from the reference program's by a relative error of at most 0.0003.
Values sent between devices are 32-bit elements; how exact they have to be, the bound alone decides.
No kernel may reach another device: no remote copies, remote signals or barrier semaphores. Data moves between devices by JAX's collectives and lax.ppermute only.
A program may use at most 64 MiB of HBM per device.

```python
import math
import jax
import jax.numpy as jnp
from jax import lax

F = 1000
K = 10
VOX = 16384
ATOMS = 262144


def draw_signals(key, part):
    key_vals, key_scale = jax.random.split(key, 2)
    values = jax.random.truncated_normal(key_vals, -6.0, 6.0, (F, VOX), jnp.float32)
    scales = jnp.exp(jax.random.uniform(key_scale, (VOX,), jnp.float32, math.log(0.3), math.log(3.0)))
    return (values * scales[None, :]).astype(jnp.bfloat16)


def levels(rng, shape, cuts, smallest, largest):
    def one(axis_at, blocks):
        heights = jax.random.uniform(jax.random.fold_in(jax.random.fold_in(rng, 6), axis_at), (blocks,), jnp.float32, smallest / len(cuts), largest / len(cuts))
        return jnp.repeat(jnp.exp(heights), shape[axis_at] // blocks).reshape((-1,) + (1,) * (len(shape) - axis_at - 1))

    gain = one(*cuts[0])
    for cut in cuts[1:]:
        gain = gain * one(*cut)
    return gain


def scatter_about(rng, shape, scale, limit, shards=(), held_as=jnp.bfloat16):
    loudness = levels(rng, shape, shards, -0.22, 0.18) if shards else 1.0
    array = jax.random.normal(rng, shape, jnp.float32) * scale * loudness
    return jnp.minimum(jnp.maximum(array, -limit), limit).astype(held_as)


def setup_inputs(seed: int = 0) -> dict:
    seeds = jax.random.split(jax.random.key(seed), 5)
    signals = draw_signals(jax.random.fold_in(seeds[4], 71), 0)
    basis = scatter_about(seeds[1], (K, F), F ** -0.5, 0.1875, ((1, 8),))
    atoms = scatter_about(seeds[2], (K, ATOMS), 1.0, 6.0, ((1, 512),), jnp.float32)
    params = jnp.clip(jax.random.uniform(seeds[3], (3, ATOMS), jnp.float32, -1.5, 1.5) * levels(seeds[3], (3, ATOMS), ((1, 512),), -0.4, 0.0), -1.5, 1.5)
    return dict(signals=signals, basis=basis, atoms=atoms, params=params)


score_scale = 1.5


def reference(signals, basis, atoms, params):
    coefficients = jnp.dot(basis, signals, preferred_element_type=jnp.float32)
    block_size = math.gcd(ATOMS, 2048)
    block_count = ATOMS // block_size
    atom_blocks = atoms.reshape(K, block_count, block_size).transpose(1, 0, 2)
    param_blocks = params.reshape(3, block_count, block_size).transpose(1, 0, 2)
    voxels = coefficients.shape[1]

    def step(running, pieces):
        run_peak, run_total, run_weighted = running
        atom_piece, param_piece = pieces
        scores = score_scale * lax.dot_general(coefficients, atom_piece, (((0,), (0,)), ((), ())), precision=lax.Precision.HIGHEST, preferred_element_type=jnp.float32)
        new_peak = jnp.maximum(run_peak, jnp.max(scores, axis=1))
        weights = jnp.exp(scores - new_peak[:, None])
        factor = jnp.exp(run_peak - new_peak)
        run_total = run_total * factor + jnp.sum(weights, axis=1)
        run_weighted = run_weighted * factor[None, :] + lax.dot_general(param_piece, weights, (((1,), (1,)), ((), ())), precision=lax.Precision.HIGHEST, preferred_element_type=jnp.float32)
        return (new_peak, run_total, run_weighted), None

    start_state = (jnp.full((voxels,), -1e30, jnp.float32), jnp.zeros((voxels,), jnp.float32), jnp.zeros((3, voxels), jnp.float32))
    final_state, unused = lax.scan(step, start_state, (atom_blocks, param_blocks))
    maps = final_state[2] / final_state[1][None, :]
    return coefficients, maps
```

```python
import functools
import math

import jax
import jax.numpy as jnp
from jax import lax
from jax.experimental import pallas as pl
from jax.experimental.pallas import tpu as pltpu
from jax.sharding import Mesh
from jax.sharding import PartitionSpec as P


scale = 1.5 * math.log2(math.e)
limit = 2.0**100

ATOM_ROWS, PARAM_ROWS, ONE_ROW, ROWS = 10, 3, 13, 16


def split(values):
    high = values.astype(jnp.bfloat16)
    rest = values - high.astype(jnp.float32)
    middle = rest.astype(jnp.bfloat16)
    low = (rest - middle.astype(jnp.float32)).astype(jnp.bfloat16)
    return high, middle, low


def match_kernel(coefs_ref, own_ref, core_ref, near_ref, far_ref, state_ref, own_coefs_ref, plain, shifted, sums, peak):
    groups = coefs_ref.shape[0] // 2
    half = coefs_ref.shape[2]
    width = 2 * half
    row = lax.broadcasted_iota(jnp.int32, (ROWS, 1), 0)

    def stack(values):
        high, middle, low = split(values)
        return jnp.concatenate([high, middle, low, high, middle, high], axis=0)

    mine = lax.axis_index("zl")
    mine_sum = coefs_ref[mine] + coefs_ref[groups + mine]
    own_coefs_ref[:, :half] = mine_sum[:ATOM_ROWS]
    own_coefs_ref[:, half:] = mine_sum[ATOM_ROWS:]

    zeros = jnp.zeros((ROWS - ATOM_ROWS, half), jnp.float32)
    for g in range(groups):
        both = scale * (coefs_ref[g] + coefs_ref[groups + g])
        for h in range(2):
            part = both[h * ATOM_ROWS : (h + 1) * ATOM_ROWS]
            at = g * width + h * half
            plain[:, at : at + half] = jnp.concatenate([part, zeros], axis=0)

    def atom_terms(piece):
        high, middle, low = split(piece)
        return jnp.concatenate([high, high, high, middle, middle, low], axis=0)

    def param_terms(piece):
        kept = jnp.where((row >= ATOM_ROWS) & (row <= ONE_ROW), piece, 0.0)
        high, middle, low = split(kept)
        rolled = (
            high.astype(jnp.float32)
            + pltpu.roll(middle.astype(jnp.float32), 6, 0)
            + pltpu.roll(low.astype(jnp.float32), 10, 0)
        )
        return rolled.astype(jnp.bfloat16)

    def scores_of(terms, stacked):
        return lax.dot_general(terms, stacked, (((0,), (0,)), ((), ())), preferred_element_type=jnp.float32)

    def weigh(params, weights):
        high = weights.astype(jnp.bfloat16)
        low = (weights - high.astype(jnp.float32)).astype(jnp.bfloat16)
        return jnp.dot(params, high, preferred_element_type=jnp.float32) + jnp.dot(
            params, low, preferred_element_type=jnp.float32
        )

    peak[...] = jnp.max(scores_of(atom_terms(own_ref[0]), stack(plain[...])), axis=0, keepdims=True)
    shifted[...] = stack(jnp.where(row == ONE_ROW, -peak[...], plain[...]))
    sums[...] = jnp.zeros_like(sums)

    def fast(pieces, i):
        piece = pieces[i]
        sums[...] += weigh(param_terms(piece), jnp.exp2(scores_of(atom_terms(piece), shifted[...])))

    def careful(pieces, i):
        piece = pieces[i]
        scores = scores_of(atom_terms(piece), stack(plain[...]))
        top = jnp.maximum(peak[...], jnp.max(scores, axis=0, keepdims=True))
        sums[...] = sums[...] * jnp.exp2(peak[...] - top) + weigh(param_terms(piece), jnp.exp2(scores - top))
        peak[...] = top

    def over_pieces(step):
        for pieces in (own_ref, core_ref, near_ref, far_ref):
            count = pieces.shape[0]
            if count == 1:
                step(pieces, 0)
            else:
                lax.fori_loop(0, count, lambda i, _, pieces=pieces: (step(pieces, i), 0)[1], 0)

    over_pieces(fast)

    fine = jnp.all(sums[ONE_ROW : ONE_ROW + 1, :] < limit)

    @pl.when(jnp.logical_not(fine))
    def _():
        sums[...] = jnp.zeros_like(sums)
        over_pieces(careful)

    total = sums[ONE_ROW : ONE_ROW + 1, :]
    weighted = sums[10:13, :] + sums[0:3, :] + sums[4:7, :]
    for g in range(groups):
        at = slice(g * width, (g + 1) * width)
        state = jnp.concatenate([peak[:, at], total[:, at], weighted[:, at], jnp.zeros((3, width), jnp.float32)], axis=0)
        state_ref[g] = state
        state_ref[groups + g] = state


def match(coefs, own, core, near, far):
    groups, voxels = coefs.shape[0] // 2, 2 * coefs.shape[2]
    everything = groups * voxels
    return pl.pallas_call(
        match_kernel,
        out_shape=(
            jax.ShapeDtypeStruct((2 * groups, 8, voxels), jnp.float32),
            jax.ShapeDtypeStruct((ATOM_ROWS, voxels), jnp.float32),
        ),
        in_specs=[pl.BlockSpec(memory_space=pltpu.VMEM)] * 5,
        out_specs=(pl.BlockSpec(memory_space=pltpu.VMEM),) * 2,
        scratch_shapes=[
            pltpu.VMEM((ROWS, everything), jnp.float32),
            pltpu.VMEM((6 * ROWS, everything), jnp.bfloat16),
            pltpu.VMEM((ROWS, everything), jnp.float32),
            pltpu.VMEM((1, everything), jnp.float32),
        ],
        name="match",
    )(coefs, own, core, near, far)


def merge(states):
    peak = jnp.max(states[:, :1], axis=0)
    factor = jnp.exp2(states[:, :1] - peak[None])
    return peak, jnp.sum(states[:, 1:5] * factor, axis=0)


def exchange(array, axis, mask):
    size = lax.axis_size(axis)
    return lax.ppermute(array, axis, [(i, i ^ mask) for i in range(size)])


def gathered(array, axes):
    count = lax.axis_size(axes)
    return lax.all_to_all(jnp.broadcast_to(array[None], (count,) + array.shape), axes, 0, 0)


def on_device(signals, basis, atoms, params):
    width = atoms.shape[1]
    half = signals.shape[1] // 2
    own = jnp.concatenate([atoms, params, jnp.ones((1, width), jnp.float32), jnp.zeros((2, width), jnp.float32)])[None]
    with jax.named_scope("core"):
        core = exchange(own, "c", 1)

    partial_sums = jnp.dot(basis, signals, preferred_element_type=jnp.float32)
    partial_sums = jnp.concatenate([partial_sums[:, :half], partial_sums[:, half:]], axis=0)

    with jax.named_scope("near"):
        near = exchange(jnp.concatenate([own, core]), "y", 1)
    with jax.named_scope("sumx"):
        sums = jnp.sum(gathered(partial_sums, "x"), axis=0)
    with jax.named_scope("far"):
        far = exchange(jnp.concatenate([own, core, near]), "y", 2)
    with jax.named_scope("allz"):
        coefs = gathered(sums, ("zh", "zl"))

    states, coefficients = match(coefs, own, core, near, far)
    with jax.named_scope("backz"):
        peak, rest = merge(lax.all_to_all(states, ("zh", "zl"), 0, 0))
    with jax.named_scope("backx"):
        state = jnp.concatenate([peak, rest, jnp.zeros((3, peak.shape[1]), jnp.float32)])
        peak, rest = merge(gathered(state, "x"))
    return coefficients, rest[1:4] / rest[:1]


def solution(mesh):
    sizes = dict(zip(("x", "zh", "y", "zl", "c"), (4, 2, 4, 8, 2)))
    fine = Mesh(mesh.devices.reshape(tuple(sizes.values())), tuple(sizes))
    af, vert = ("x", "zh"), ("y", "zl", "c")
    return jax.shard_map(
        on_device,
        mesh=fine,
        in_specs=(P(af, vert), P(None, af), P(None, af + vert), P(None, af + vert)),
        out_specs=(P(None, vert), P(None, vert)),
        check_vma=False,
    )
```

```python
import math

import jax
import jax.numpy as jnp
from jax import lax
from jax.experimental import pallas as pl
from jax.experimental.pallas import tpu as pltpu
from jax.sharding import Mesh
from jax.sharding import PartitionSpec as P


scale = 1.5 * math.log2(math.e)
limit = 2.0**100

ATOM_ROWS, ONE_ROW, ROWS = 10, 13, 16


def split(values):
    high = values.astype(jnp.bfloat16)
    rest = values - high.astype(jnp.float32)
    middle = rest.astype(jnp.bfloat16)
    low = (rest - middle.astype(jnp.float32)).astype(jnp.bfloat16)
    return high, middle, low


def unpack_kernel(coefs_ref, plain_ref, own_coefs_ref):
    groups = coefs_ref.shape[0] // 2
    half = coefs_ref.shape[2]
    mine = lax.axis_index("zl")
    mine_sum = coefs_ref[mine] + coefs_ref[groups + mine]
    own_coefs_ref[:, :half] = mine_sum[:ATOM_ROWS]
    own_coefs_ref[:, half:] = mine_sum[ATOM_ROWS:]

    zeros = jnp.zeros((ROWS - ATOM_ROWS, half), jnp.float32)
    for g in range(groups):
        both = scale * (coefs_ref[g] + coefs_ref[groups + g])
        for h in range(2):
            part = both[h * ATOM_ROWS : (h + 1) * ATOM_ROWS]
            at = (2 * g + h) * half
            plain_ref[:, at : at + half] = jnp.concatenate([part, zeros], axis=0)


def match_kernel(plain, own_ref, core_ref, near_ref, far_ref, state_ref, shifted, sums, peak):
    groups = state_ref.shape[0] // 2
    width = state_ref.shape[2]
    row = lax.broadcasted_iota(jnp.int32, (ROWS, 1), 0)

    def stack(values):
        high, middle, low = split(values)
        return jnp.concatenate([high, middle, low, high, middle, high], axis=0)

    def atom_terms(piece):
        high, middle, low = split(piece)
        return jnp.concatenate([high, high, high, middle, middle, low], axis=0)

    def param_terms(piece):
        kept = jnp.where((row >= ATOM_ROWS) & (row <= ONE_ROW), piece, 0.0)
        high, middle, low = split(kept)
        rolled = (
            high.astype(jnp.float32)
            + pltpu.roll(middle.astype(jnp.float32), 6, 0)
            + pltpu.roll(low.astype(jnp.float32), 10, 0)
        )
        return rolled.astype(jnp.bfloat16)

    def scores_of(terms, stacked):
        return lax.dot_general(terms, stacked, (((0,), (0,)), ((), ())), preferred_element_type=jnp.float32)

    def weigh(params, weights):
        high = weights.astype(jnp.bfloat16)
        low = (weights - high.astype(jnp.float32)).astype(jnp.bfloat16)
        return jnp.dot(params, high, preferred_element_type=jnp.float32) + jnp.dot(
            params, low, preferred_element_type=jnp.float32
        )

    peak[...] = jnp.max(scores_of(atom_terms(own_ref[0]), stack(plain[...])), axis=0, keepdims=True)
    shifted[...] = stack(jnp.where(row == ONE_ROW, -peak[...], plain[...]))
    sums[...] = jnp.zeros_like(sums)

    def fast(pieces, i):
        piece = pieces[i]
        sums[...] += weigh(param_terms(piece), jnp.exp2(scores_of(atom_terms(piece), shifted[...])))

    def careful(pieces, i):
        piece = pieces[i]
        scores = scores_of(atom_terms(piece), stack(plain[...]))
        top = jnp.maximum(peak[...], jnp.max(scores, axis=0, keepdims=True))
        sums[...] = sums[...] * jnp.exp2(peak[...] - top) + weigh(param_terms(piece), jnp.exp2(scores - top))
        peak[...] = top

    def over_pieces(step):
        for pieces in (own_ref, core_ref, near_ref, far_ref):
            count = pieces.shape[0]
            if count == 1:
                step(pieces, 0)
            else:
                lax.fori_loop(0, count, lambda i, _, pieces=pieces: (step(pieces, i), 0)[1], 0)

    over_pieces(fast)

    fine = jnp.all(sums[ONE_ROW : ONE_ROW + 1, :] < limit)

    @pl.when(jnp.logical_not(fine))
    def _():
        sums[...] = jnp.zeros_like(sums)
        over_pieces(careful)

    total = sums[ONE_ROW : ONE_ROW + 1, :]
    weighted = sums[10:13, :] + sums[0:3, :] + sums[4:7, :]
    for g in range(groups):
        at = slice(g * width, (g + 1) * width)
        state = jnp.concatenate([peak[:, at], total[:, at], weighted[:, at], jnp.zeros((3, width), jnp.float32)], axis=0)
        state_ref[g] = state
        state_ref[groups + g] = state


def match(plain, own, core, near, far, groups):
    everything = plain.shape[1]
    return pl.pallas_call(
        match_kernel,
        out_shape=shape(2 * groups, 8, everything // groups),
        in_specs=[pl.BlockSpec(memory_space=pltpu.VMEM)] * 5,
        out_specs=pl.BlockSpec(memory_space=pltpu.VMEM),
        scratch_shapes=[
            pltpu.VMEM((6 * ROWS, everything), jnp.bfloat16),
            pltpu.VMEM((ROWS, everything), jnp.float32),
            pltpu.VMEM((1, everything), jnp.float32),
        ],
        compiler_params=pltpu.CompilerParams(vmem_limit_bytes=24 << 20),
        name="match",
    )(plain, own, core, near, far)


def call(kernel, shapes, *arrays):
    return pl.pallas_call(
        kernel,
        out_shape=shapes,
        in_specs=[pl.BlockSpec(memory_space=pltpu.VMEM)] * len(arrays),
        out_specs=jax.tree.map(lambda _: pl.BlockSpec(memory_space=pltpu.VMEM), shapes),
        compiler_params=pltpu.CompilerParams(vmem_limit_bytes=4 << 20),
    )(*arrays)


def pack_kernel(atoms_ref, params_ref, own_ref):
    own_ref[0, :ATOM_ROWS] = atoms_ref[...]
    own_ref[0, ATOM_ROWS:ONE_ROW] = params_ref[...]
    own_ref[0, ONE_ROW : ONE_ROW + 1] = jnp.ones((1, atoms_ref.shape[1]), jnp.float32)
    own_ref[0, ONE_ROW + 1 :] = jnp.zeros((ROWS - ONE_ROW - 1, atoms_ref.shape[1]), jnp.float32)


def project_kernel(basis_ref, signals_ref, out_ref):
    sums = jnp.dot(basis_ref[...], signals_ref[...], preferred_element_type=jnp.float32)
    half = sums.shape[1] // 2
    for i in range(out_ref.shape[0]):
        out_ref[i, :ATOM_ROWS] = sums[:, :half]
        out_ref[i, ATOM_ROWS:] = sums[:, half:]


def add_kernel(parts_ref, out_ref):
    total = jnp.sum(parts_ref[...], axis=0)
    for i in range(out_ref.shape[0]):
        out_ref[i] = total


def merged(states):
    peak = jnp.max(states[:, :1], axis=0)
    return peak, jnp.sum(states * jnp.exp2(states[:, :1] - peak[None]), axis=0)


def merge_kernel(states_ref, out_ref):
    peak, sums = merged(states_ref[...])
    row = lax.broadcasted_iota(jnp.int32, sums.shape, 0)
    state = jnp.where(row == 0, peak, sums)
    for i in range(out_ref.shape[0]):
        out_ref[i] = state


def finish_kernel(states_ref, maps_ref):
    _, sums = merged(states_ref[...])
    maps_ref[...] = sums[2:5] / sums[1:2]


def shape(*sizes):
    return jax.ShapeDtypeStruct(sizes, jnp.float32)


def exchange(array, axis, mask):
    return lax.ppermute(array, axis, [(i, i ^ mask) for i in range(lax.axis_size(axis))])


def on_device(signals, basis, atoms, params):
    width, voxels = atoms.shape[1], signals.shape[1]
    across, along = lax.axis_size("x"), lax.axis_size(("zh", "zl"))
    own = call(pack_kernel, shape(1, ROWS, width), atoms, params)
    core = exchange(own, "c", 1)
    sums = call(project_kernel, shape(across, 2 * ATOM_ROWS, voxels // 2), basis, signals)
    near = exchange(jnp.concatenate([own, core]), "y", 1)
    sums = lax.all_to_all(sums, "x", 0, 0)
    sums = call(add_kernel, shape(along, 2 * ATOM_ROWS, voxels // 2), sums)
    far = exchange(jnp.concatenate([own, core, near]), "y", 2)
    coefs = lax.all_to_all(sums, ("zh", "zl"), 0, 0)

    groups = along // 2
    plain, coefficients = call(unpack_kernel, (shape(ROWS, groups * voxels), shape(ATOM_ROWS, voxels)), coefs)
    states = match(plain, own, core, near, far, groups)
    states = lax.all_to_all(states, ("zh", "zl"), 0, 0)
    states = call(merge_kernel, shape(across, 8, voxels), states)
    states = lax.all_to_all(states, "x", 0, 0)
    maps = call(finish_kernel, shape(3, voxels), states)
    return coefficients, maps


def solution(mesh):
    sizes = dict(zip(("x", "zh", "y", "zl", "c"), (4, 2, 4, 8, 2)))
    fine = Mesh(mesh.devices.reshape(tuple(sizes.values())), tuple(sizes))
    af, vert = ("x", "zh"), ("y", "zl", "c")
    return jax.shard_map(
        on_device,
        mesh=fine,
        in_specs=(P(af, vert), P(None, af), P(None, af + vert), P(None, af + vert)),
        out_specs=(P(None, vert), P(None, vert)),
        check_vma=False,
    )
```

```python
import math

import jax
import jax.numpy as jnp
from jax import lax
from jax.experimental import pallas as pl
from jax.experimental.pallas import tpu as pltpu
from jax.sharding import Mesh
from jax.sharding import PartitionSpec as P


scale = 1.5 * math.log2(math.e)
limit = 2.0**100

ATOM_ROWS, ONE_ROW, ROWS = 10, 13, 16


def split(values):
    high = values.astype(jnp.bfloat16)
    rest = values - high.astype(jnp.float32)
    middle = rest.astype(jnp.bfloat16)
    low = (rest - middle.astype(jnp.float32)).astype(jnp.bfloat16)
    return high, middle, low


def stack(values):
    high, middle, low = split(values)
    return jnp.concatenate([high, middle, low, high, middle, high], axis=0)


def atom_terms(piece):
    high, middle, low = split(piece)
    return jnp.concatenate([high, high, high, middle, middle, low], axis=0)


def row_index():
    return lax.broadcasted_iota(jnp.int32, (ROWS, 1), 0)


def param_terms(piece):
    row = row_index()
    kept = jnp.where((row >= ATOM_ROWS) & (row <= ONE_ROW), piece, 0.0)
    high, middle, low = split(kept)
    rolled = (
        high.astype(jnp.float32)
        + pltpu.roll(middle.astype(jnp.float32), 6, 0)
        + pltpu.roll(low.astype(jnp.float32), 10, 0)
    )
    return rolled.astype(jnp.bfloat16)


def scores_of(terms, stacked):
    return lax.dot_general(terms, stacked, (((0,), (0,)), ((), ())), preferred_element_type=jnp.float32)


def weigh(params, weights):
    high = weights.astype(jnp.bfloat16)
    low = (weights - high.astype(jnp.float32)).astype(jnp.bfloat16)
    return jnp.dot(params, high, preferred_element_type=jnp.float32) + jnp.dot(
        params, low, preferred_element_type=jnp.float32
    )


def over_pieces(refs, step):
    for pieces in refs:
        count = pieces.shape[0]
        if count == 1:
            step(pieces, 0)
        else:
            lax.fori_loop(0, count, lambda i, _, pieces=pieces: (step(pieces, i), 0)[1], 0)


def add_weights(refs, shifted, sums):
    def step(pieces, i):
        piece = pieces[i]
        sums[...] += weigh(param_terms(piece), jnp.exp2(scores_of(atom_terms(piece), shifted[...])))

    over_pieces(refs, step)


def begin_kernel(coefs_ref, own_ref, core_ref, near_ref, plain, shifted, peak, sums, own_coefs_ref, kept, sem):
    groups = coefs_ref.shape[0] // 2
    half = coefs_ref.shape[2]
    mine = lax.axis_index("zl")
    mine_sum = coefs_ref[mine] + coefs_ref[groups + mine]
    kept[:, :half] = mine_sum[:ATOM_ROWS]
    kept[:, half:] = mine_sum[ATOM_ROWS:]
    copy = pltpu.make_async_copy(kept, own_coefs_ref, sem)
    copy.start()

    zeros = jnp.zeros((ROWS - ATOM_ROWS, half), jnp.float32)
    for g in range(groups):
        both = scale * (coefs_ref[g] + coefs_ref[groups + g])
        for h in range(2):
            part = both[h * ATOM_ROWS : (h + 1) * ATOM_ROWS]
            at = (2 * g + h) * half
            plain[:, at : at + half] = jnp.concatenate([part, zeros], axis=0)

    peak[...] = jnp.max(scores_of(atom_terms(own_ref[0]), stack(plain[...])), axis=0, keepdims=True)
    shifted[...] = stack(jnp.where(row_index() == ONE_ROW, -peak[...], plain[...]))
    sums[...] = jnp.zeros_like(sums)
    add_weights((own_ref, core_ref, near_ref), shifted, sums)
    copy.wait()


def end_kernel(plain, shifted, first_peak, first_sums, own_ref, core_ref, near_ref, far_ref, state_ref, peak, sums):
    groups = state_ref.shape[0] // 2
    width = state_ref.shape[2]
    peak[...] = first_peak[...]
    sums[...] = first_sums[...]
    add_weights((far_ref,), shifted, sums)
    fine = jnp.all(sums[ONE_ROW : ONE_ROW + 1, :] < limit)

    @pl.when(jnp.logical_not(fine))
    def _():
        sums[...] = jnp.zeros_like(sums)

        def step(pieces, i):
            piece = pieces[i]
            scores = scores_of(atom_terms(piece), stack(plain[...]))
            top = jnp.maximum(peak[...], jnp.max(scores, axis=0, keepdims=True))
            sums[...] = sums[...] * jnp.exp2(peak[...] - top) + weigh(param_terms(piece), jnp.exp2(scores - top))
            peak[...] = top

        over_pieces((own_ref, core_ref, near_ref, far_ref), step)

    total = sums[ONE_ROW : ONE_ROW + 1, :]
    weighted = sums[10:13, :] + sums[0:3, :] + sums[4:7, :]
    for g in range(groups):
        at = slice(g * width, (g + 1) * width)
        state = jnp.concatenate([peak[:, at], total[:, at], weighted[:, at], jnp.zeros((3, width), jnp.float32)], axis=0)
        state_ref[g] = state
        state_ref[groups + g] = state


def in_vmem():
    return pl.BlockSpec(memory_space=pltpu.VMEM)


def begin(coefs, own, core, near):
    groups, voxels = coefs.shape[0] // 2, 2 * coefs.shape[2]
    everything = groups * voxels
    return pl.pallas_call(
        begin_kernel,
        out_shape=(
            shape(ROWS, everything),
            jax.ShapeDtypeStruct((6 * ROWS, everything), jnp.bfloat16),
            shape(1, everything),
            shape(ROWS, everything),
            shape(ATOM_ROWS, voxels),
        ),
        in_specs=[in_vmem()] * 4,
        out_specs=(in_vmem(),) * 4 + (pl.BlockSpec(memory_space=pl.ANY),),
        scratch_shapes=[pltpu.VMEM((ATOM_ROWS, voxels), jnp.float32), pltpu.SemaphoreType.DMA],
        compiler_params=pltpu.CompilerParams(vmem_limit_bytes=24 << 20),
        name="begin",
    )(coefs, own, core, near)


def end(groups, plain, *rest):
    everything = plain.shape[1]
    return pl.pallas_call(
        end_kernel,
        out_shape=shape(2 * groups, 8, everything // groups),
        in_specs=[in_vmem()] * 8,
        out_specs=in_vmem(),
        scratch_shapes=[pltpu.VMEM((1, everything), jnp.float32), pltpu.VMEM((ROWS, everything), jnp.float32)],
        compiler_params=pltpu.CompilerParams(vmem_limit_bytes=24 << 20),
        name="end",
    )(plain, *rest)


def call(kernel, shapes, *arrays):
    return pl.pallas_call(
        kernel,
        out_shape=shapes,
        in_specs=[pl.BlockSpec(memory_space=pltpu.VMEM)] * len(arrays),
        out_specs=jax.tree.map(lambda _: pl.BlockSpec(memory_space=pltpu.VMEM), shapes),
        compiler_params=pltpu.CompilerParams(vmem_limit_bytes=4 << 20),
    )(*arrays)


def pack_kernel(atoms_ref, params_ref, own_ref):
    own_ref[0, :ATOM_ROWS] = atoms_ref[...]
    own_ref[0, ATOM_ROWS:ONE_ROW] = params_ref[...]
    own_ref[0, ONE_ROW : ONE_ROW + 1] = jnp.ones((1, atoms_ref.shape[1]), jnp.float32)
    own_ref[0, ONE_ROW + 1 :] = jnp.zeros((ROWS - ONE_ROW - 1, atoms_ref.shape[1]), jnp.float32)


def project_kernel(basis_ref, signals_ref, out_ref):
    sums = jnp.dot(basis_ref[...], signals_ref[...], preferred_element_type=jnp.float32)
    half = sums.shape[1] // 2
    for i in range(out_ref.shape[0]):
        out_ref[i, :ATOM_ROWS] = sums[:, :half]
        out_ref[i, ATOM_ROWS:] = sums[:, half:]


def add_kernel(parts_ref, out_ref):
    total = jnp.sum(parts_ref[...], axis=0)
    for i in range(out_ref.shape[0]):
        out_ref[i] = total


def merged(states):
    peak = jnp.max(states[:, :1], axis=0)
    return peak, jnp.sum(states * jnp.exp2(states[:, :1] - peak[None]), axis=0)


def merge_kernel(states_ref, out_ref):
    peak, sums = merged(states_ref[...])
    row = lax.broadcasted_iota(jnp.int32, sums.shape, 0)
    state = jnp.where(row == 0, peak, sums)
    for i in range(out_ref.shape[0]):
        out_ref[i] = state


def finish_kernel(states_ref, maps_ref):
    _, sums = merged(states_ref[...])
    maps_ref[...] = sums[2:5] / sums[1:2]


def shape(*sizes):
    return jax.ShapeDtypeStruct(sizes, jnp.float32)


def exchange(array, axis, mask):
    return lax.ppermute(array, axis, [(i, i ^ mask) for i in range(lax.axis_size(axis))])


def on_device(signals, basis, atoms, params):
    width, voxels = atoms.shape[1], signals.shape[1]
    across, along = lax.axis_size("x"), lax.axis_size(("zh", "zl"))
    sums = call(project_kernel, shape(across, 2 * ATOM_ROWS, voxels // 2), basis, signals)
    own = call(pack_kernel, shape(1, ROWS, width), atoms, params)
    sums = lax.all_to_all(sums, "x", 0, 0)
    core = exchange(own, "c", 1)
    sums = call(add_kernel, shape(along, 2 * ATOM_ROWS, voxels // 2), sums)
    coefs = lax.all_to_all(sums, ("zh", "zl"), 0, 0)
    near = exchange(jnp.concatenate([own, core]), "y", 1)
    far = exchange(jnp.concatenate([own, core, near]), "y", 2)

    groups = along // 2
    plain, shifted, peak, sums, coefficients = begin(coefs, own, core, near)
    states = end(groups, plain, shifted, peak, sums, own, core, near, far)
    states = lax.all_to_all(states, ("zh", "zl"), 0, 0)
    states = call(merge_kernel, shape(across, 8, voxels), states)
    states = lax.all_to_all(states, "x", 0, 0)
    maps = call(finish_kernel, shape(3, voxels), states)
    return coefficients, maps


def solution(mesh):
    sizes = dict(zip(("x", "zh", "y", "zl", "c"), (4, 2, 4, 8, 2)))
    fine = Mesh(mesh.devices.reshape(tuple(sizes.values())), tuple(sizes))
    af, vert = ("x", "zh"), ("y", "zl", "c")
    return jax.shard_map(
        on_device,
        mesh=fine,
        in_specs=(P(af, vert), P(None, af), P(None, af + vert), P(None, af + vert)),
        out_specs=(P(None, vert), P(None, vert)),
        check_vma=False,
    )
```

```python
import math

import jax
import jax.numpy as jnp
from jax import lax
from jax.experimental import pallas as pl
from jax.experimental.pallas import tpu as pltpu
from jax.sharding import Mesh
from jax.sharding import PartitionSpec as P


scale = 1.5 * math.log2(math.e)
limit = 2.0**100

ATOM_ROWS, ONE_ROW, ROWS = 10, 13, 16
PACKED, STATES = 5, 5


def split(values):
    high = values.astype(jnp.bfloat16)
    rest = values - high.astype(jnp.float32)
    middle = rest.astype(jnp.bfloat16)
    low = (rest - middle.astype(jnp.float32)).astype(jnp.bfloat16)
    return high, middle, low


def stack(values):
    high, middle, low = split(values)
    return jnp.concatenate([high, middle, low, high, middle, high], axis=0)


def atom_terms(piece):
    high, middle, low = split(piece)
    return jnp.concatenate([high, high, high, middle, middle, low], axis=0)


def row_index():
    return lax.broadcasted_iota(jnp.int32, (ROWS, 1), 0)


def param_terms(piece):
    row = row_index()
    kept = jnp.where((row >= ATOM_ROWS) & (row <= ONE_ROW), piece, 0.0)
    high, middle, low = split(kept)
    rolled = (
        high.astype(jnp.float32)
        + pltpu.roll(middle.astype(jnp.float32), 6, 0)
        + pltpu.roll(low.astype(jnp.float32), 10, 0)
    )
    return rolled.astype(jnp.bfloat16)


def scores_of(terms, stacked):
    return lax.dot_general(terms, stacked, (((0,), (0,)), ((), ())), preferred_element_type=jnp.float32)


def weigh(params, weights):
    high = weights.astype(jnp.bfloat16)
    low = (weights - high.astype(jnp.float32)).astype(jnp.bfloat16)
    return jnp.dot(params, high, preferred_element_type=jnp.float32) + jnp.dot(
        params, low, preferred_element_type=jnp.float32
    )


def over_pieces(refs, step):
    for pieces in refs:
        count = pieces.shape[0]
        if count == 1:
            step(pieces, 0)
        else:
            lax.fori_loop(0, count, lambda i, _, pieces=pieces: (step(pieces, i), 0)[1], 0)


def add_weights(refs, shifted, sums):
    def step(pieces, i):
        piece = pieces[i]
        sums[...] += weigh(param_terms(piece), jnp.exp2(scores_of(atom_terms(piece), shifted[...])))

    over_pieces(refs, step)


def begin_kernel(coefs_ref, own_ref, core_ref, near_ref, plain, shifted, peak, sums, own_coefs_ref, kept, sem):
    groups = coefs_ref.shape[0] // 2
    half = coefs_ref.shape[3]

    def rows_of(at):
        return jnp.concatenate([coefs_ref[at, r] + coefs_ref[groups + at, r] for r in range(PACKED)], axis=0)

    mine = rows_of(lax.axis_index("zl"))
    kept[:, :half] = mine[:ATOM_ROWS]
    kept[:, half:] = mine[ATOM_ROWS:]
    copy = pltpu.make_async_copy(kept, own_coefs_ref, sem)
    copy.start()

    zeros = jnp.zeros((ROWS - ATOM_ROWS, half), jnp.float32)
    for g in range(groups):
        both = scale * rows_of(g)
        for h in range(2):
            part = both[h * ATOM_ROWS : (h + 1) * ATOM_ROWS]
            at = (2 * g + h) * half
            plain[:, at : at + half] = jnp.concatenate([part, zeros], axis=0)

    peak[...] = jnp.max(scores_of(atom_terms(own_ref[0]), stack(plain[...])), axis=0, keepdims=True)
    shifted[...] = stack(jnp.where(row_index() == ONE_ROW, -peak[...], plain[...]))
    sums[...] = jnp.zeros_like(sums)
    add_weights((own_ref, core_ref, near_ref), shifted, sums)
    copy.wait()


def end_kernel(plain, shifted, first_peak, first_sums, own_ref, core_ref, near_ref, second_ref, third_ref, state_ref, peak, sums):
    groups = state_ref.shape[0] // 2
    half = state_ref.shape[3]
    peak[...] = first_peak[...]
    sums[...] = first_sums[...]
    add_weights((second_ref, third_ref), shifted, sums)
    fine = jnp.all(sums[ONE_ROW : ONE_ROW + 1, :] < limit)

    @pl.when(jnp.logical_not(fine))
    def _():
        sums[...] = jnp.zeros_like(sums)

        def step(pieces, i):
            piece = pieces[i]
            scores = scores_of(atom_terms(piece), stack(plain[...]))
            top = jnp.maximum(peak[...], jnp.max(scores, axis=0, keepdims=True))
            sums[...] = sums[...] * jnp.exp2(peak[...] - top) + weigh(param_terms(piece), jnp.exp2(scores - top))
            peak[...] = top

        over_pieces((own_ref, core_ref, near_ref, second_ref, third_ref), step)

    total = sums[ONE_ROW : ONE_ROW + 1, :]
    weighted = sums[10:13, :] + sums[0:3, :] + sums[4:7, :]
    values = (peak[...], total, weighted[0:1], weighted[1:2], weighted[2:3])
    for g in range(groups):
        for i, value in enumerate(values):
            for h in range(2):
                at = (2 * g + h) * half
                row = value[:, at : at + half]
                state_ref[g, i, h : h + 1] = row
                state_ref[groups + g, i, h : h + 1] = row


def in_vmem():
    return pl.BlockSpec(memory_space=pltpu.VMEM)


def begin(coefs, own, core, near):
    groups, voxels = coefs.shape[0] // 2, 2 * coefs.shape[3]
    everything = groups * voxels
    return pl.pallas_call(
        begin_kernel,
        out_shape=(
            shape(ROWS, everything),
            jax.ShapeDtypeStruct((6 * ROWS, everything), jnp.bfloat16),
            shape(1, everything),
            shape(ROWS, everything),
            shape(ATOM_ROWS, voxels),
        ),
        in_specs=[in_vmem()] * 4,
        out_specs=(in_vmem(),) * 4 + (pl.BlockSpec(memory_space=pl.ANY),),
        scratch_shapes=[pltpu.VMEM((ATOM_ROWS, voxels), jnp.float32), pltpu.SemaphoreType.DMA],
        compiler_params=pltpu.CompilerParams(vmem_limit_bytes=24 << 20),
        name="begin",
    )(coefs, own, core, near)


def end(groups, plain, *rest):
    everything = plain.shape[1]
    return pl.pallas_call(
        end_kernel,
        out_shape=shape(2 * groups, STATES, 2, everything // groups // 2),
        in_specs=[in_vmem()] * 9,
        out_specs=in_vmem(),
        scratch_shapes=[pltpu.VMEM((1, everything), jnp.float32), pltpu.VMEM((ROWS, everything), jnp.float32)],
        compiler_params=pltpu.CompilerParams(vmem_limit_bytes=24 << 20),
        name="end",
    )(plain, *rest)


def call(kernel, shapes, *arrays):
    return pl.pallas_call(
        kernel,
        out_shape=shapes,
        in_specs=[pl.BlockSpec(memory_space=pltpu.VMEM)] * len(arrays),
        out_specs=jax.tree.map(lambda _: pl.BlockSpec(memory_space=pltpu.VMEM), shapes),
        compiler_params=pltpu.CompilerParams(vmem_limit_bytes=4 << 20),
    )(*arrays)


def pack_kernel(atoms_ref, params_ref, own_ref):
    own_ref[0, :ATOM_ROWS] = atoms_ref[...]
    own_ref[0, ATOM_ROWS:ONE_ROW] = params_ref[...]
    own_ref[0, ONE_ROW : ONE_ROW + 1] = jnp.ones((1, atoms_ref.shape[1]), jnp.float32)
    own_ref[0, ONE_ROW + 1 :] = jnp.zeros((ROWS - ONE_ROW - 1, atoms_ref.shape[1]), jnp.float32)


def project_kernel(basis_ref, signals_ref, out_ref):
    sums = jnp.dot(basis_ref[...], signals_ref[...], preferred_element_type=jnp.float32)
    half = sums.shape[1] // 2
    rows = jnp.concatenate([sums[:, :half], sums[:, half:]], axis=0)
    for i in range(out_ref.shape[0]):
        for r in range(PACKED):
            out_ref[i, r] = rows[4 * r : 4 * r + 4]


def add_kernel(parts_ref, out_ref):
    total = jnp.sum(parts_ref[...], axis=0)
    for i in range(out_ref.shape[0]):
        out_ref[i] = total


def merged(states):
    peak = jnp.max(states[:, 0], axis=0)
    factors = jnp.exp2(states[:, 0] - peak[None])
    return [peak] + [jnp.sum(states[:, i] * factors, axis=0) for i in range(1, STATES)]


def merge_kernel(states_ref, out_ref):
    state = merged(states_ref[...])
    for i in range(out_ref.shape[0]):
        for j in range(STATES):
            out_ref[i, j] = state[j]


def finish_kernel(states_ref, maps_ref):
    _, total, *weighted = merged(states_ref[...])
    half = total.shape[1]
    for j, value in enumerate(weighted):
        result = value / total
        for h in range(2):
            maps_ref[j : j + 1, h * half : (h + 1) * half] = result[h : h + 1]


def shape(*sizes):
    return jax.ShapeDtypeStruct(sizes, jnp.float32)


def exchange(array, axis, mask):
    return lax.ppermute(array, axis, [(i, i ^ mask) for i in range(lax.axis_size(axis))])


def on_device(signals, basis, atoms, params):
    width, half = atoms.shape[1], signals.shape[1] // 2
    across, along = lax.axis_size("x"), lax.axis_size(("zh", "zl"))
    sums = call(project_kernel, shape(across, PACKED, 4, half), basis, signals)
    own = call(pack_kernel, shape(1, ROWS, width), atoms, params)
    sums = lax.all_to_all(sums, "x", 0, 0)
    core = exchange(own, "c", 1)
    sums = call(add_kernel, shape(along, PACKED, 4, half), sums)
    coefs = lax.all_to_all(sums, ("zh", "zl"), 0, 0)
    both = jnp.concatenate([own, core])
    near = exchange(both, "y", 1)
    second = exchange(both, "y", 2)
    third = exchange(both, "y", 3)

    groups = along // 2
    plain, shifted, peak, sums, coefficients = begin(coefs, own, core, near)
    states = end(groups, plain, shifted, peak, sums, own, core, near, second, third)
    states = lax.all_to_all(states, ("zh", "zl"), 0, 0)
    states = call(merge_kernel, shape(across, STATES, 2, half), states)
    states = lax.all_to_all(states, "x", 0, 0)
    maps = call(finish_kernel, shape(3, 2 * half), states)
    return coefficients, maps


def solution(mesh):
    sizes = dict(zip(("x", "zh", "y", "zl", "c"), (4, 2, 4, 8, 2)))
    fine = Mesh(mesh.devices.reshape(tuple(sizes.values())), tuple(sizes))
    af, vert = ("x", "zh"), ("y", "zl", "c")
    return jax.shard_map(
        on_device,
        mesh=fine,
        in_specs=(P(af, vert), P(None, af), P(None, af + vert), P(None, af + vert)),
        out_specs=(P(None, vert), P(None, vert)),
        check_vma=False,
    )
```

```python
import math

import jax
import jax.numpy as jnp
from jax import lax
from jax.experimental import pallas as pl
from jax.experimental.pallas import tpu as pltpu
from jax.sharding import Mesh
from jax.sharding import PartitionSpec as P


scale = 1.5 * math.log2(math.e)
limit = 2.0**100

ATOM_ROWS, ONE_ROW, ROWS = 10, 13, 16
PACKED, STATES = 5, 5
COEFS_FROM, STATES_FROM = 12, 8
SAMPLE = 128


def split(values):
    high = values.astype(jnp.bfloat16)
    rest = values - high.astype(jnp.float32)
    middle = rest.astype(jnp.bfloat16)
    low = (rest - middle.astype(jnp.float32)).astype(jnp.bfloat16)
    return high, middle, low


def stack(values):
    high, middle, low = split(values)
    return jnp.concatenate([high, middle, low, high, middle, high], axis=0)


def atom_terms(piece):
    high, middle, low = split(piece)
    return jnp.concatenate([high, high, high, middle, middle, low], axis=0)


def row_index():
    return lax.broadcasted_iota(jnp.int32, (ROWS, 1), 0)


def param_terms(piece):
    row = row_index()
    kept = jnp.where((row >= ATOM_ROWS) & (row <= ONE_ROW), piece, 0.0)
    high, middle, low = split(kept)
    rolled = (
        high.astype(jnp.float32)
        + pltpu.roll(middle.astype(jnp.float32), 6, 0)
        + pltpu.roll(low.astype(jnp.float32), 10, 0)
    )
    return rolled.astype(jnp.bfloat16)


def scores_of(terms, stacked):
    return lax.dot_general(terms, stacked, (((0,), (0,)), ((), ())), preferred_element_type=jnp.float32)


def weigh(params, weights):
    high = weights.astype(jnp.bfloat16)
    low = (weights - high.astype(jnp.float32)).astype(jnp.bfloat16)
    return jnp.dot(params, high, preferred_element_type=jnp.float32) + jnp.dot(
        params, low, preferred_element_type=jnp.float32
    )


def over_pieces(refs, step):
    for pieces in refs:
        count = pieces.shape[0]
        if count == 1:
            step(pieces, 0)
        else:
            lax.fori_loop(0, count, lambda i, _, pieces=pieces: (step(pieces, i), 0)[1], 0)


def add_weights(refs, shifted, sums):
    def step(pieces, i):
        piece = pieces[i]
        sums[...] += weigh(param_terms(piece), jnp.exp2(scores_of(atom_terms(piece), shifted[...])))

    over_pieces(refs, step)


def begin_kernel(coefs_ref, mine_ref, plain, shifted, peak, sums, own_coefs_ref, kept, sem):
    groups = coefs_ref.shape[0] // 2
    half = coefs_ref.shape[3]

    def rows_of(zl):
        at = (zl + 2 * groups - COEFS_FROM) % groups
        return jnp.concatenate([coefs_ref[at, r] + coefs_ref[groups + at, r] for r in range(PACKED)], axis=0)

    mine = rows_of(lax.axis_index("zl"))
    kept[:, :half] = mine[:ATOM_ROWS]
    kept[:, half:] = mine[ATOM_ROWS:]
    copy = pltpu.make_async_copy(kept, own_coefs_ref, sem)
    copy.start()

    zeros = jnp.zeros((ROWS - ATOM_ROWS, half), jnp.float32)
    for g in range(groups):
        both = scale * rows_of(g)
        for h in range(2):
            part = both[h * ATOM_ROWS : (h + 1) * ATOM_ROWS]
            at = (2 * g + h) * half
            plain[:, at : at + half] = jnp.concatenate([part, zeros], axis=0)

    peak[...] = jnp.max(scores_of(atom_terms(mine_ref[0])[:, :SAMPLE], stack(plain[...])), axis=0, keepdims=True)
    shifted[...] = stack(jnp.where(row_index() == ONE_ROW, -peak[...], plain[...]))
    sums[...] = jnp.zeros_like(sums)
    add_weights((mine_ref,), shifted, sums)
    copy.wait()


def end_kernel(plain, shifted, first_peak, first_sums, mine_ref, theirs_ref, state_ref, peak, sums):
    groups = state_ref.shape[0] // 2
    half = state_ref.shape[3]
    peak[...] = first_peak[...]
    sums[...] = first_sums[...]
    add_weights((theirs_ref,), shifted, sums)
    fine = jnp.all(sums[ONE_ROW : ONE_ROW + 1, :] < limit)

    @pl.when(jnp.logical_not(fine))
    def _():
        sums[...] = jnp.zeros_like(sums)

        def step(pieces, i):
            piece = pieces[i]
            scores = scores_of(atom_terms(piece), stack(plain[...]))
            top = jnp.maximum(peak[...], jnp.max(scores, axis=0, keepdims=True))
            sums[...] = sums[...] * jnp.exp2(peak[...] - top) + weigh(param_terms(piece), jnp.exp2(scores - top))
            peak[...] = top

        over_pieces((mine_ref, theirs_ref), step)

    total = sums[ONE_ROW : ONE_ROW + 1, :]
    weighted = sums[10:13, :] + sums[0:3, :] + sums[4:7, :]
    values = (peak[...], total, weighted[0:1], weighted[1:2], weighted[2:3])
    for g in range(groups):
        for i, value in enumerate(values):
            for h in range(2):
                at = (2 * g + h) * half
                row = value[:, at : at + half]
                slot = (g - STATES_FROM) % groups
                state_ref[slot, i, h : h + 1] = row
                state_ref[groups + slot, i, h : h + 1] = row


def in_vmem():
    return pl.BlockSpec(memory_space=pltpu.VMEM)


def begin(coefs, mine):
    groups, voxels = coefs.shape[0] // 2, 2 * coefs.shape[3]
    everything = groups * voxels
    return pl.pallas_call(
        begin_kernel,
        out_shape=(
            shape(ROWS, everything),
            jax.ShapeDtypeStruct((6 * ROWS, everything), jnp.bfloat16),
            shape(1, everything),
            shape(ROWS, everything),
            shape(ATOM_ROWS, voxels),
        ),
        in_specs=[in_vmem()] * 2,
        out_specs=(in_vmem(),) * 4 + (pl.BlockSpec(memory_space=pl.ANY),),
        scratch_shapes=[pltpu.VMEM((ATOM_ROWS, voxels), jnp.float32), pltpu.SemaphoreType.DMA],
        compiler_params=pltpu.CompilerParams(vmem_limit_bytes=24 << 20),
        name="begin",
    )(coefs, mine)


def end(groups, plain, *rest):
    everything = plain.shape[1]
    return pl.pallas_call(
        end_kernel,
        out_shape=shape(2 * groups, STATES, 2, everything // groups // 2),
        in_specs=[in_vmem()] * 6,
        out_specs=in_vmem(),
        scratch_shapes=[pltpu.VMEM((1, everything), jnp.float32), pltpu.VMEM((ROWS, everything), jnp.float32)],
        compiler_params=pltpu.CompilerParams(vmem_limit_bytes=24 << 20),
        name="end",
    )(plain, *rest)


def call(kernel, shapes, *arrays):
    return pl.pallas_call(
        kernel,
        out_shape=shapes,
        in_specs=[in_vmem()] * len(arrays),
        out_specs=jax.tree.map(lambda _: in_vmem(), shapes),
        compiler_params=pltpu.CompilerParams(vmem_limit_bytes=4 << 20),
    )(*arrays)


def pack_kernel(atoms_ref, params_ref, own_ref):
    width = atoms_ref.shape[1]
    own_ref[0, :ATOM_ROWS] = atoms_ref[...]
    own_ref[0, ATOM_ROWS:ONE_ROW] = params_ref[...]
    own_ref[0, ONE_ROW : ONE_ROW + 1] = jnp.ones((1, width), jnp.float32)
    own_ref[0, ONE_ROW + 1 :] = jnp.zeros((ROWS - ONE_ROW - 1, width), jnp.float32)


def project_kernel(signals_ref, basis_ref, out_ref, signals, basis, sems):
    copies = [
        pltpu.make_async_copy(signals_ref, signals, sems.at[0]),
        pltpu.make_async_copy(basis_ref, basis, sems.at[1]),
    ]
    for copy in copies:
        copy.start()
    for copy in copies:
        copy.wait()
    sums = jnp.dot(basis[...], signals[...], preferred_element_type=jnp.float32)
    half = sums.shape[1] // 2
    rows = jnp.concatenate([sums[:, :half], sums[:, half:]], axis=0)
    for r in range(PACKED):
        block = rows[4 * r : 4 * r + 4]
        for i in range(out_ref.shape[0]):
            out_ref[i, r] = block


def project(signals, basis, slots):
    arrays = [pltpu.with_memory_space_constraint(array, pltpu.HBM) for array in (signals, basis)]
    return pl.pallas_call(
        project_kernel,
        out_shape=shape(slots, PACKED, 4, signals.shape[1] // 2),
        in_specs=[pl.BlockSpec(memory_space=pltpu.HBM)] * 2,
        out_specs=in_vmem(),
        scratch_shapes=[pltpu.VMEM(array.shape, array.dtype) for array in arrays] + [pltpu.SemaphoreType.DMA((2,))],
        compiler_params=pltpu.CompilerParams(vmem_limit_bytes=4 << 20),
        name="project",
    )(*arrays)


def add_kernel(parts_ref, out_ref):
    total = jnp.sum(parts_ref[...], axis=0)
    for i in range(out_ref.shape[0]):
        out_ref[i] = total


def merged(states):
    peak = jnp.max(states[:, 0], axis=0)
    factors = jnp.exp2(states[:, 0] - peak[None])
    return [peak] + [jnp.sum(states[:, i] * factors, axis=0) for i in range(1, STATES)]


def merge_kernel(states_ref, out_ref):
    state = merged(states_ref[...])
    for i in range(out_ref.shape[0]):
        for j in range(STATES):
            out_ref[i, j] = state[j]


def finish_kernel(states_ref, maps_ref):
    _, total, *weighted = merged(states_ref[...])
    half = total.shape[1]
    for j, value in enumerate(weighted):
        result = value / total
        for h in range(2):
            maps_ref[j : j + 1, h * half : (h + 1) * half] = result[h : h + 1]


def shape(*sizes):
    return jax.ShapeDtypeStruct(sizes, jnp.float32)


def exchange(array, axis, mask):
    return lax.ppermute(array, axis, [(i, i ^ mask) for i in range(lax.axis_size(axis))])


def spread(array, axes):
    order = [0]
    for axis in axes:
        size = lax.axis_size(axis)
        order = [at * size + (i + size // 2) % size for at in order for i in range(size)]
    return lax.all_to_all(array, axes, 0, 0, axis_index_groups=[order])


def along_z(array, first):
    count = lax.axis_size(("zh", "zl"))
    order = [(i + first) % count for i in range(count)]
    return lax.all_to_all(array, ("zh", "zl"), 0, 0, axis_index_groups=[order])


def on_device(signals, basis, atoms, params):
    width, half = atoms.shape[1], signals.shape[1] // 2
    across, along = lax.axis_size("x"), lax.axis_size(("zh", "zl"))
    sums = project(signals, basis, across)
    sums = spread(sums, ("x",))
    own = call(pack_kernel, shape(1, ROWS, width), atoms, params)
    near = exchange(own, "y", 1)
    sums = call(add_kernel, shape(along, PACKED, 4, half), sums)
    coefs = along_z(sums, COEFS_FROM)
    pair = jnp.concatenate([own, near])
    far = exchange(pair, "y", 2)
    mine = jnp.concatenate([pair, far])
    theirs = exchange(mine, "c", 1)

    groups = along // 2
    plain, shifted, peak, sums, coefficients = begin(coefs, mine)
    states = end(groups, plain, shifted, peak, sums, mine, theirs)
    states = along_z(states, STATES_FROM)
    states = call(merge_kernel, shape(across, STATES, 2, half), states)
    states = spread(states, ("x",))
    maps = call(finish_kernel, shape(3, 2 * half), states)
    return coefficients, maps


def solution(mesh):
    sizes = dict(zip(("x", "zh", "y", "zl", "c"), (4, 2, 4, 8, 2)))
    fine = Mesh(mesh.devices.reshape(tuple(sizes.values())), tuple(sizes))
    af, vert = ("x", "zh"), ("y", "zl", "c")
    return jax.shard_map(
        on_device,
        mesh=fine,
        in_specs=(P(af, vert), P(None, af), P(None, af + vert), P(None, af + vert)),
        out_specs=(P(None, vert), P(None, vert)),
        check_vma=False,
    )
```

```python
import math

import jax
import jax.numpy as jnp
from jax import lax
from jax.experimental import pallas as pl
from jax.experimental.pallas import tpu as pltpu
from jax.sharding import Mesh
from jax.sharding import PartitionSpec as P


scale = 1.5 * math.log2(math.e)
margin, limit = 80.0, 2.0**120

ATOM_ROWS, ONE_ROW, ROWS = 10, 13, 16
PACKED, STATES = 5, 5
COEFS_FROM, STATES_FROM = 10, 8
SAMPLE = 128


def split(values):
    high = values.astype(jnp.bfloat16)
    rest = values - high.astype(jnp.float32)
    middle = rest.astype(jnp.bfloat16)
    low = (rest - middle.astype(jnp.float32)).astype(jnp.bfloat16)
    return high, middle, low


def stack(values):
    high, middle, low = split(values)
    return jnp.concatenate([high, middle, low, high, middle, high], axis=0)


def atom_terms(piece):
    high, middle, low = split(piece)
    return jnp.concatenate([high, high, high, middle, middle, low], axis=0)


def row_index():
    return lax.broadcasted_iota(jnp.int32, (ROWS, 1), 0)


def param_terms(piece):
    row = row_index()
    kept = jnp.where((row >= ATOM_ROWS) & (row <= ONE_ROW), piece, 0.0)
    high, middle, low = split(kept)
    rolled = (
        high.astype(jnp.float32)
        + pltpu.roll(middle.astype(jnp.float32), 6, 0)
        + pltpu.roll(low.astype(jnp.float32), 10, 0)
    )
    return rolled.astype(jnp.bfloat16)


def scores_of(terms, stacked):
    return lax.dot_general(terms, stacked, (((0,), (0,)), ((), ())), preferred_element_type=jnp.float32)


def weigh(params, weights):
    high = weights.astype(jnp.bfloat16)
    low = (weights - high.astype(jnp.float32)).astype(jnp.bfloat16)
    return jnp.dot(params, high, preferred_element_type=jnp.float32) + jnp.dot(
        params, low, preferred_element_type=jnp.float32
    )


def over_pieces(refs, step):
    for pieces in refs:
        count = pieces.shape[0]
        if count == 1:
            step(pieces, 0)
        else:
            lax.fori_loop(0, count, lambda i, _, pieces=pieces: (step(pieces, i), 0)[1], 0)


def add_weights(refs, shifted, sums):
    def step(pieces, i):
        piece = pieces[i]
        sums[...] += weigh(param_terms(piece), jnp.exp2(scores_of(atom_terms(piece), shifted[...])))

    over_pieces(refs, step)


def begin_kernel(coefs_ref, near_ref, plain, shifted, peak, sums, own_coefs_ref, kept, sem):
    groups = coefs_ref.shape[0] // 2
    half = coefs_ref.shape[3]

    def rows_of(zl):
        at = (zl + 2 * groups - COEFS_FROM) % groups
        return jnp.concatenate([coefs_ref[at, r] + coefs_ref[groups + at, r] for r in range(PACKED)], axis=0)

    mine = rows_of(lax.axis_index("zl"))
    kept[:, :half] = mine[:ATOM_ROWS]
    kept[:, half:] = mine[ATOM_ROWS:]
    copy = pltpu.make_async_copy(kept, own_coefs_ref, sem)
    copy.start()

    zeros = jnp.zeros((ROWS - ATOM_ROWS, half), jnp.float32)
    for g in range(groups):
        both = scale * rows_of(g)
        for h in range(2):
            part = both[h * ATOM_ROWS : (h + 1) * ATOM_ROWS]
            at = (2 * g + h) * half
            plain[:, at : at + half] = jnp.concatenate([part, zeros], axis=0)

    sample = scores_of(atom_terms(near_ref[0])[:, :SAMPLE], stack(plain[...]))
    peak[...] = margin + jnp.max(sample, axis=0, keepdims=True)
    shifted[...] = stack(jnp.where(row_index() == ONE_ROW, -peak[...], plain[...]))
    sums[...] = jnp.zeros_like(sums)
    add_weights((near_ref,), shifted, sums)
    copy.wait()


def end_kernel(plain, shifted, first_peak, first_sums, near_ref, far_ref, state_ref, peak, sums):
    groups = state_ref.shape[0] // 2
    half = state_ref.shape[3]
    peak[...] = first_peak[...]
    sums[...] = first_sums[...]
    add_weights((far_ref,), shifted, sums)
    fine = jnp.all(sums[ONE_ROW : ONE_ROW + 1, :] < limit)

    @pl.when(jnp.logical_not(fine))
    def _():
        sums[...] = jnp.zeros_like(sums)

        def step(pieces, i):
            piece = pieces[i]
            scores = scores_of(atom_terms(piece), stack(plain[...]))
            top = jnp.maximum(peak[...], jnp.max(scores, axis=0, keepdims=True))
            sums[...] = sums[...] * jnp.exp2(peak[...] - top) + weigh(param_terms(piece), jnp.exp2(scores - top))
            peak[...] = top

        over_pieces((near_ref, far_ref), step)

    total = sums[ONE_ROW : ONE_ROW + 1, :]
    shift = jnp.round(jnp.log2(total))
    down = jnp.exp2(-shift)
    weighted = (sums[10:13, :] + sums[0:3, :] + sums[4:7, :]) * down
    values = (peak[...] + shift, total * down, weighted[0:1], weighted[1:2], weighted[2:3])
    for g in range(groups):
        for i, value in enumerate(values):
            for h in range(2):
                at = (2 * g + h) * half
                row = value[:, at : at + half]
                slot = (g - STATES_FROM) % groups
                state_ref[slot, i, h : h + 1] = row
                state_ref[groups + slot, i, h : h + 1] = row


def in_vmem():
    return pl.BlockSpec(memory_space=pltpu.VMEM)


def begin(coefs, mine):
    groups, voxels = coefs.shape[0] // 2, 2 * coefs.shape[3]
    everything = groups * voxels
    return pl.pallas_call(
        begin_kernel,
        out_shape=(
            shape(ROWS, everything),
            jax.ShapeDtypeStruct((6 * ROWS, everything), jnp.bfloat16),
            shape(1, everything),
            shape(ROWS, everything),
            shape(ATOM_ROWS, voxels),
        ),
        in_specs=[in_vmem()] * 2,
        out_specs=(in_vmem(),) * 4 + (pl.BlockSpec(memory_space=pl.ANY),),
        scratch_shapes=[pltpu.VMEM((ATOM_ROWS, voxels), jnp.float32), pltpu.SemaphoreType.DMA],
        compiler_params=pltpu.CompilerParams(vmem_limit_bytes=24 << 20),
        name="begin",
    )(coefs, mine)


def end(groups, plain, *rest):
    everything = plain.shape[1]
    return pl.pallas_call(
        end_kernel,
        out_shape=shape(2 * groups, STATES, 2, everything // groups // 2),
        in_specs=[in_vmem()] * 6,
        out_specs=in_vmem(),
        scratch_shapes=[pltpu.VMEM((1, everything), jnp.float32), pltpu.VMEM((ROWS, everything), jnp.float32)],
        compiler_params=pltpu.CompilerParams(vmem_limit_bytes=24 << 20),
        name="end",
    )(plain, *rest)


def call(kernel, shapes, *arrays):
    return pl.pallas_call(
        kernel,
        out_shape=shapes,
        in_specs=[in_vmem()] * len(arrays),
        out_specs=jax.tree.map(lambda _: in_vmem(), shapes),
        compiler_params=pltpu.CompilerParams(vmem_limit_bytes=4 << 20),
    )(*arrays)


def pack_kernel(atoms_ref, params_ref, own_ref):
    width = atoms_ref.shape[1]
    own_ref[0, :ATOM_ROWS] = atoms_ref[...]
    own_ref[0, ATOM_ROWS:ONE_ROW] = params_ref[...]
    own_ref[0, ONE_ROW : ONE_ROW + 1] = jnp.ones((1, width), jnp.float32)
    own_ref[0, ONE_ROW + 1 :] = jnp.zeros((ROWS - ONE_ROW - 1, width), jnp.float32)


def project_kernel(signals_ref, basis_ref, out_ref, signals, basis, sems):
    copies = [
        pltpu.make_async_copy(signals_ref, signals, sems.at[0]),
        pltpu.make_async_copy(basis_ref, basis, sems.at[1]),
    ]
    for copy in copies:
        copy.start()
    for copy in copies:
        copy.wait()
    sums = jnp.dot(basis[...], signals[...], preferred_element_type=jnp.float32)
    half = sums.shape[1] // 2
    rows = jnp.concatenate([sums[:, :half], sums[:, half:]], axis=0)
    for r in range(PACKED):
        block = rows[4 * r : 4 * r + 4]
        for i in range(out_ref.shape[0]):
            out_ref[i, r] = block


def project(signals, basis, slots):
    arrays = [pltpu.with_memory_space_constraint(array, pltpu.HBM) for array in (signals, basis)]
    return pl.pallas_call(
        project_kernel,
        out_shape=shape(slots, PACKED, 4, signals.shape[1] // 2),
        in_specs=[pl.BlockSpec(memory_space=pltpu.HBM)] * 2,
        out_specs=in_vmem(),
        scratch_shapes=[pltpu.VMEM(array.shape, array.dtype) for array in arrays] + [pltpu.SemaphoreType.DMA((2,))],
        compiler_params=pltpu.CompilerParams(vmem_limit_bytes=4 << 20),
        name="project",
    )(*arrays)


def add_kernel(parts_ref, out_ref):
    total = jnp.sum(parts_ref[...], axis=0)
    for i in range(out_ref.shape[0]):
        out_ref[i] = total


def merged(states):
    peak = jnp.max(states[:, 0], axis=0)
    factors = jnp.exp2(states[:, 0] - peak[None])
    return [peak] + [jnp.sum(states[:, i] * factors, axis=0) for i in range(1, STATES)]


def merge_kernel(states_ref, out_ref):
    state = merged(states_ref[...])
    for i in range(out_ref.shape[0]):
        for j in range(STATES):
            out_ref[i, j] = state[j]


def finish_kernel(states_ref, maps_ref):
    _, total, *weighted = merged(states_ref[...])
    half = total.shape[1]
    for j, value in enumerate(weighted):
        result = value / total
        for h in range(2):
            maps_ref[j : j + 1, h * half : (h + 1) * half] = result[h : h + 1]


def shape(*sizes):
    return jax.ShapeDtypeStruct(sizes, jnp.float32)


def exchange(array, axis, mask):
    return lax.ppermute(array, axis, [(i, i ^ mask) for i in range(lax.axis_size(axis))])


def spread(array, axes):
    order = [0]
    for axis in axes:
        size = lax.axis_size(axis)
        order = [at * size + (i + size // 2) % size for at in order for i in range(size)]
    return lax.all_to_all(array, axes, 0, 0, axis_index_groups=[order])


def along_z(array, first):
    count = lax.axis_size(("zh", "zl"))
    order = [(i + first) % count for i in range(count)]
    return lax.all_to_all(array, ("zh", "zl"), 0, 0, axis_index_groups=[order])


def on_device(signals, basis, atoms, params):
    width, half = atoms.shape[1], signals.shape[1] // 2
    across, along = lax.axis_size("x"), lax.axis_size(("zh", "zl"))
    sums = project(signals, basis, across)
    sums = spread(sums, ("x",))
    own = call(pack_kernel, shape(1, ROWS, width), atoms, params)
    near = exchange(own, "y", 1)
    sums = call(add_kernel, shape(along, PACKED, 4, half), sums)
    coefs = along_z(sums, COEFS_FROM)
    pair = jnp.concatenate([own, near])
    core = exchange(pair, "c", 1)
    four = jnp.concatenate([pair, core])
    far = exchange(four, "y", 2)

    groups = along // 2
    plain, shifted, peak, sums, coefficients = begin(coefs, four)
    states = end(groups, plain, shifted, peak, sums, four, far)
    states = along_z(states, STATES_FROM)
    states = call(merge_kernel, shape(across, STATES, 2, half), states)
    states = spread(states, ("x",))
    maps = call(finish_kernel, shape(3, 2 * half), states)
    return coefficients, maps


def solution(mesh):
    sizes = dict(zip(("x", "zh", "y", "zl", "c"), (4, 2, 4, 8, 2)))
    fine = Mesh(mesh.devices.reshape(tuple(sizes.values())), tuple(sizes))
    af, vert = ("x", "zh"), ("y", "zl", "c")
    return jax.shard_map(
        on_device,
        mesh=fine,
        in_specs=(P(af, vert), P(None, af), P(None, af + vert), P(None, af + vert)),
        out_specs=(P(None, vert), P(None, vert)),
        check_vma=False,
    )
```

```python
import math

import jax
import jax.numpy as jnp
from jax import lax
from jax.experimental import pallas as pl
from jax.experimental.pallas import tpu as pltpu
from jax.sharding import Mesh
from jax.sharding import PartitionSpec as P


scale = 1.5 * math.log2(math.e)
margin, limit = 80.0, 2.0**120

ATOM_ROWS, ONE_ROW, ROWS = 10, 13, 16
PACKED, STATES = 5, 5
COEFS_FROM, STATES_FROM = 10, 8
SAMPLE = 128
TILE = 1024


def split(values):
    high = values.astype(jnp.bfloat16)
    rest = values - high.astype(jnp.float32)
    middle = rest.astype(jnp.bfloat16)
    low = (rest - middle.astype(jnp.float32)).astype(jnp.bfloat16)
    return high, middle, low


def stack(values):
    high, middle, low = split(values)
    return jnp.concatenate([high, middle, low, high, middle, high], axis=0)


def atom_terms(piece):
    high, middle, low = split(piece)
    return jnp.concatenate([high, high, high, middle, middle, low], axis=0)


def row_index():
    return lax.broadcasted_iota(jnp.int32, (ROWS, 1), 0)


def param_terms(piece):
    row = row_index()
    kept = jnp.where((row >= ATOM_ROWS) & (row <= ONE_ROW), piece, 0.0)
    high, middle, low = split(kept)
    rolled = (
        high.astype(jnp.float32)
        + pltpu.roll(middle.astype(jnp.float32), 6, 0)
        + pltpu.roll(low.astype(jnp.float32), 10, 0)
    )
    return rolled.astype(jnp.bfloat16)


def scores_of(terms, stacked):
    return lax.dot_general(terms, stacked, (((0,), (0,)), ((), ())), preferred_element_type=jnp.float32)


def weigh(params, weights):
    high = weights.astype(jnp.bfloat16)
    low = (weights - high.astype(jnp.float32)).astype(jnp.bfloat16)
    return jnp.dot(params, high, preferred_element_type=jnp.float32) + jnp.dot(
        params, low, preferred_element_type=jnp.float32
    )


def over_pieces(refs, step):
    for pieces in refs:
        count = pieces.shape[0]
        if count == 1:
            step(pieces, 0)
        else:
            lax.fori_loop(0, count, lambda i, _, pieces=pieces: (step(pieces, i), 0)[1], 0)


def add_weights(pieces, shifted, sums):
    everything = shifted.shape[1]
    for i in range(pieces.shape[0]):
        piece = pieces[i]
        atoms, params = atom_terms(piece), param_terms(piece)
        for at in range(0, everything, TILE):
            tile = slice(at, at + TILE)
            sums[:, tile] += weigh(params, jnp.exp2(scores_of(atoms, shifted[:, tile])))


def begin_kernel(coefs_ref, near_ref, plain, shifted, peak, sums, own_coefs_ref, kept, sem):
    groups = coefs_ref.shape[0] // 2
    half = coefs_ref.shape[3]

    def rows_of(zl):
        at = (zl + 2 * groups - COEFS_FROM) % groups
        return jnp.concatenate([coefs_ref[at, r] + coefs_ref[groups + at, r] for r in range(PACKED)], axis=0)

    mine = rows_of(lax.axis_index("zl"))
    kept[:, :half] = mine[:ATOM_ROWS]
    kept[:, half:] = mine[ATOM_ROWS:]
    copy = pltpu.make_async_copy(kept, own_coefs_ref, sem)
    copy.start()

    zeros = jnp.zeros((ROWS - ATOM_ROWS, half), jnp.float32)
    for g in range(groups):
        both = scale * rows_of(g)
        for h in range(2):
            part = both[h * ATOM_ROWS : (h + 1) * ATOM_ROWS]
            at = (2 * g + h) * half
            plain[:, at : at + half] = jnp.concatenate([part, zeros], axis=0)

    sample = scores_of(atom_terms(near_ref[0])[:, :SAMPLE], stack(plain[...]))
    peak[...] = margin + jnp.max(sample, axis=0, keepdims=True)
    shifted[...] = stack(jnp.where(row_index() == ONE_ROW, -peak[...], plain[...]))
    sums[...] = jnp.zeros_like(sums)
    add_weights(near_ref, shifted, sums)
    copy.wait()


def end_kernel(plain, shifted, first_peak, first_sums, near_ref, far_ref, state_ref, peak, sums):
    groups = state_ref.shape[0] // 2
    half = state_ref.shape[3]
    peak[...] = first_peak[...]
    sums[...] = first_sums[...]
    add_weights(far_ref, shifted, sums)
    fine = jnp.all(sums[ONE_ROW : ONE_ROW + 1, :] < limit)

    @pl.when(jnp.logical_not(fine))
    def _():
        sums[...] = jnp.zeros_like(sums)

        def step(pieces, i):
            piece = pieces[i]
            scores = scores_of(atom_terms(piece), stack(plain[...]))
            top = jnp.maximum(peak[...], jnp.max(scores, axis=0, keepdims=True))
            sums[...] = sums[...] * jnp.exp2(peak[...] - top) + weigh(param_terms(piece), jnp.exp2(scores - top))
            peak[...] = top

        over_pieces((near_ref, far_ref), step)

    total = sums[ONE_ROW : ONE_ROW + 1, :]
    shift = jnp.round(jnp.log2(total))
    down = jnp.exp2(-shift)
    weighted = (sums[10:13, :] + sums[0:3, :] + sums[4:7, :]) * down
    values = (peak[...] + shift, total * down, weighted[0:1], weighted[1:2], weighted[2:3])
    for g in range(groups):
        for i, value in enumerate(values):
            for h in range(2):
                at = (2 * g + h) * half
                row = value[:, at : at + half]
                slot = (g - STATES_FROM) % groups
                state_ref[slot, i, h : h + 1] = row
                state_ref[groups + slot, i, h : h + 1] = row


def in_vmem():
    return pl.BlockSpec(memory_space=pltpu.VMEM)


def begin(coefs, mine):
    groups, voxels = coefs.shape[0] // 2, 2 * coefs.shape[3]
    everything = groups * voxels
    return pl.pallas_call(
        begin_kernel,
        out_shape=(
            shape(ROWS, everything),
            jax.ShapeDtypeStruct((6 * ROWS, everything), jnp.bfloat16),
            shape(1, everything),
            shape(ROWS, everything),
            shape(ATOM_ROWS, voxels),
        ),
        in_specs=[in_vmem()] * 2,
        out_specs=(in_vmem(),) * 4 + (pl.BlockSpec(memory_space=pl.ANY),),
        scratch_shapes=[pltpu.VMEM((ATOM_ROWS, voxels), jnp.float32), pltpu.SemaphoreType.DMA],
        compiler_params=pltpu.CompilerParams(vmem_limit_bytes=24 << 20),
        name="begin",
    )(coefs, mine)


def end(groups, plain, *rest):
    everything = plain.shape[1]
    return pl.pallas_call(
        end_kernel,
        out_shape=shape(2 * groups, STATES, 2, everything // groups // 2),
        in_specs=[in_vmem()] * 6,
        out_specs=in_vmem(),
        scratch_shapes=[pltpu.VMEM((1, everything), jnp.float32), pltpu.VMEM((ROWS, everything), jnp.float32)],
        compiler_params=pltpu.CompilerParams(vmem_limit_bytes=24 << 20),
        name="end",
    )(plain, *rest)


def call(kernel, shapes, *arrays):
    return pl.pallas_call(
        kernel,
        out_shape=shapes,
        in_specs=[in_vmem()] * len(arrays),
        out_specs=jax.tree.map(lambda _: in_vmem(), shapes),
        compiler_params=pltpu.CompilerParams(vmem_limit_bytes=4 << 20),
    )(*arrays)


def pack_kernel(atoms_ref, params_ref, own_ref):
    width = atoms_ref.shape[1]
    own_ref[0, :ATOM_ROWS] = atoms_ref[...]
    own_ref[0, ATOM_ROWS:ONE_ROW] = params_ref[...]
    own_ref[0, ONE_ROW : ONE_ROW + 1] = jnp.ones((1, width), jnp.float32)
    own_ref[0, ONE_ROW + 1 :] = jnp.zeros((ROWS - ONE_ROW - 1, width), jnp.float32)


def project_kernel(signals_ref, basis_ref, out_ref, signals, basis, sems):
    copies = [
        pltpu.make_async_copy(signals_ref, signals, sems.at[0]),
        pltpu.make_async_copy(basis_ref, basis, sems.at[1]),
    ]
    for copy in copies:
        copy.start()
    for copy in copies:
        copy.wait()
    sums = jnp.dot(basis[...], signals[...], preferred_element_type=jnp.float32)
    half = sums.shape[1] // 2
    rows = jnp.concatenate([sums[:, :half], sums[:, half:]], axis=0)
    for r in range(PACKED):
        block = rows[4 * r : 4 * r + 4]
        for i in range(out_ref.shape[0]):
            out_ref[i, r] = block


def project(signals, basis, slots):
    arrays = [pltpu.with_memory_space_constraint(array, pltpu.HBM) for array in (signals, basis)]
    return pl.pallas_call(
        project_kernel,
        out_shape=shape(slots, PACKED, 4, signals.shape[1] // 2),
        in_specs=[pl.BlockSpec(memory_space=pltpu.HBM)] * 2,
        out_specs=in_vmem(),
        scratch_shapes=[pltpu.VMEM(array.shape, array.dtype) for array in arrays] + [pltpu.SemaphoreType.DMA((2,))],
        compiler_params=pltpu.CompilerParams(vmem_limit_bytes=4 << 20),
        name="project",
    )(*arrays)


def add_kernel(parts_ref, out_ref):
    total = jnp.sum(parts_ref[...], axis=0)
    for i in range(out_ref.shape[0]):
        out_ref[i] = total


def merged(states):
    peak = jnp.max(states[:, 0], axis=0)
    factors = jnp.exp2(states[:, 0] - peak[None])
    return [peak] + [jnp.sum(states[:, i] * factors, axis=0) for i in range(1, STATES)]


def merge_kernel(states_ref, out_ref):
    state = merged(states_ref[...])
    for i in range(out_ref.shape[0]):
        for j in range(STATES):
            out_ref[i, j] = state[j]


def finish_kernel(states_ref, maps_ref):
    _, total, *weighted = merged(states_ref[...])
    half = total.shape[1]
    for j, value in enumerate(weighted):
        result = value / total
        for h in range(2):
            maps_ref[j : j + 1, h * half : (h + 1) * half] = result[h : h + 1]


def shape(*sizes):
    return jax.ShapeDtypeStruct(sizes, jnp.float32)


def exchange(array, axis, mask):
    return lax.ppermute(array, axis, [(i, i ^ mask) for i in range(lax.axis_size(axis))])


def spread(array, axes):
    order = [0]
    for axis in axes:
        size = lax.axis_size(axis)
        order = [at * size + (i + size // 2) % size for at in order for i in range(size)]
    return lax.all_to_all(array, axes, 0, 0, axis_index_groups=[order])


def along_z(array, first):
    count = lax.axis_size(("zh", "zl"))
    order = [(i + first) % count for i in range(count)]
    return lax.all_to_all(array, ("zh", "zl"), 0, 0, axis_index_groups=[order])


def on_device(signals, basis, atoms, params):
    width, half = atoms.shape[1], signals.shape[1] // 2
    across, along = lax.axis_size("x"), lax.axis_size(("zh", "zl"))
    sums = project(signals, basis, across)
    sums = spread(sums, ("x",))
    own = call(pack_kernel, shape(1, ROWS, width), atoms, params)
    near = exchange(own, "y", 1)
    sums = call(add_kernel, shape(along, PACKED, 4, half), sums)
    coefs = along_z(sums, COEFS_FROM)
    pair = jnp.concatenate([own, near])
    core = exchange(pair, "c", 1)
    four = jnp.concatenate([pair, core])
    far = exchange(four, "y", 2)

    groups = along // 2
    plain, shifted, peak, sums, coefficients = begin(coefs, four)
    states = end(groups, plain, shifted, peak, sums, four, far)
    states = along_z(states, STATES_FROM)
    states = call(merge_kernel, shape(across, STATES, 2, half), states)
    states = spread(states, ("x",))
    maps = call(finish_kernel, shape(3, 2 * half), states)
    return coefficients, maps


def solution(mesh):
    sizes = dict(zip(("x", "zh", "y", "zl", "c"), (4, 2, 4, 8, 2)))
    fine = Mesh(mesh.devices.reshape(tuple(sizes.values())), tuple(sizes))
    af, vert = ("x", "zh"), ("y", "zl", "c")
    return jax.shard_map(
        on_device,
        mesh=fine,
        in_specs=(P(af, vert), P(None, af), P(None, af + vert), P(None, af + vert)),
        out_specs=(P(None, vert), P(None, vert)),
        check_vma=False,
    )
```

```python
import math

import jax
import jax.numpy as jnp
from jax import lax
from jax.experimental import pallas as pl
from jax.experimental.pallas import tpu as pltpu
from jax.sharding import Mesh
from jax.sharding import PartitionSpec as P


scale = 1.5 * math.log2(math.e)
margin, limit = 80.0, 2.0**120

ATOM_ROWS, ONE_ROW, ROWS = 10, 13, 16
PACKED, STATES = 5, 5
COEFS_FROM, STATES_FROM = 10, 8
SAMPLE = 128
TILE = 1024


def split(values):
    high = values.astype(jnp.bfloat16)
    rest = values - high.astype(jnp.float32)
    middle = rest.astype(jnp.bfloat16)
    low = (rest - middle.astype(jnp.float32)).astype(jnp.bfloat16)
    return high, middle, low


def stack(values):
    high, middle, low = split(values)
    return jnp.concatenate([high, middle, low, high, middle, high], axis=0)


def atom_terms(piece):
    high, middle, low = split(piece)
    return jnp.concatenate([high, high, high, middle, middle, low], axis=0)


def row_index():
    return lax.broadcasted_iota(jnp.int32, (ROWS, 1), 0)


def param_terms(piece):
    row = row_index()
    kept = jnp.where((row >= ATOM_ROWS) & (row <= ONE_ROW), piece, 0.0)
    high, middle, low = split(kept)
    rolled = (
        high.astype(jnp.float32)
        + pltpu.roll(middle.astype(jnp.float32), 6, 0)
        + pltpu.roll(low.astype(jnp.float32), 10, 0)
    )
    return rolled.astype(jnp.bfloat16)


def scores_of(terms, stacked):
    return lax.dot_general(terms, stacked, (((0,), (0,)), ((), ())), preferred_element_type=jnp.float32)


def weigh(params, weights):
    high = weights.astype(jnp.bfloat16)
    low = (weights - high.astype(jnp.float32)).astype(jnp.bfloat16)
    twice, both = jnp.concatenate([params, params], axis=1), jnp.concatenate([high, low], axis=0)
    return jnp.dot(twice, both, preferred_element_type=jnp.float32)


def over_pieces(refs, step):
    for pieces in refs:
        count = pieces.shape[0]
        if count == 1:
            step(pieces, 0)
        else:
            lax.fori_loop(0, count, lambda i, _, pieces=pieces: (step(pieces, i), 0)[1], 0)


def add_weights(pieces, shifted, sums):
    everything = shifted.shape[1]
    for i in range(pieces.shape[0]):
        piece = pieces[i]
        atoms, params = atom_terms(piece), param_terms(piece)
        for at in range(0, everything, TILE):
            tile = slice(at, at + TILE)
            sums[:, tile] += weigh(params, jnp.exp2(scores_of(atoms, shifted[:, tile])))


def begin_kernel(coefs_ref, near_ref, plain, shifted, peak, sums, own_coefs_ref, kept, sem):
    groups = coefs_ref.shape[0] // 2
    half = coefs_ref.shape[3]

    def rows_of(zl):
        at = (zl + 2 * groups - COEFS_FROM) % groups
        return jnp.concatenate([coefs_ref[at, r] + coefs_ref[groups + at, r] for r in range(PACKED)], axis=0)

    mine = rows_of(lax.axis_index("zl"))
    kept[:, :half] = mine[:ATOM_ROWS]
    kept[:, half:] = mine[ATOM_ROWS:]
    copy = pltpu.make_async_copy(kept, own_coefs_ref, sem)
    copy.start()

    zeros = jnp.zeros((ROWS - ATOM_ROWS, half), jnp.float32)
    for g in range(groups):
        both = scale * rows_of(g)
        for h in range(2):
            part = both[h * ATOM_ROWS : (h + 1) * ATOM_ROWS]
            at = (2 * g + h) * half
            plain[:, at : at + half] = jnp.concatenate([part, zeros], axis=0)

    sample = scores_of(atom_terms(near_ref[0])[:, :SAMPLE], stack(plain[...]))
    peak[...] = margin + jnp.max(sample, axis=0, keepdims=True)
    shifted[...] = stack(jnp.where(row_index() == ONE_ROW, -peak[...], plain[...]))
    sums[...] = jnp.zeros_like(sums)
    add_weights(near_ref, shifted, sums)
    copy.wait()


def end_kernel(plain, shifted, first_peak, first_sums, near_ref, far_ref, state_ref, peak, sums):
    groups = state_ref.shape[0] // 2
    half = state_ref.shape[3]
    peak[...] = first_peak[...]
    sums[...] = first_sums[...]
    add_weights(far_ref, shifted, sums)
    fine = jnp.all(sums[ONE_ROW : ONE_ROW + 1, :] < limit)

    @pl.when(jnp.logical_not(fine))
    def _():
        sums[...] = jnp.zeros_like(sums)

        def step(pieces, i):
            piece = pieces[i]
            scores = scores_of(atom_terms(piece), stack(plain[...]))
            top = jnp.maximum(peak[...], jnp.max(scores, axis=0, keepdims=True))
            sums[...] = sums[...] * jnp.exp2(peak[...] - top) + weigh(param_terms(piece), jnp.exp2(scores - top))
            peak[...] = top

        over_pieces((near_ref, far_ref), step)

    total = sums[ONE_ROW : ONE_ROW + 1, :]
    shift = jnp.round(jnp.log2(total))
    down = jnp.exp2(-shift)
    weighted = (sums[10:13, :] + sums[0:3, :] + sums[4:7, :]) * down
    values = (peak[...] + shift, total * down, weighted[0:1], weighted[1:2], weighted[2:3])
    for g in range(groups):
        for i, value in enumerate(values):
            for h in range(2):
                at = (2 * g + h) * half
                row = value[:, at : at + half]
                slot = (g - STATES_FROM) % groups
                state_ref[slot, i, h : h + 1] = row
                state_ref[groups + slot, i, h : h + 1] = row


def in_vmem():
    return pl.BlockSpec(memory_space=pltpu.VMEM)


def begin(coefs, mine):
    groups, voxels = coefs.shape[0] // 2, 2 * coefs.shape[3]
    everything = groups * voxels
    return pl.pallas_call(
        begin_kernel,
        out_shape=(
            shape(ROWS, everything),
            jax.ShapeDtypeStruct((6 * ROWS, everything), jnp.bfloat16),
            shape(1, everything),
            shape(ROWS, everything),
            shape(ATOM_ROWS, voxels),
        ),
        in_specs=[in_vmem()] * 2,
        out_specs=(in_vmem(),) * 4 + (pl.BlockSpec(memory_space=pl.ANY),),
        scratch_shapes=[pltpu.VMEM((ATOM_ROWS, voxels), jnp.float32), pltpu.SemaphoreType.DMA],
        compiler_params=pltpu.CompilerParams(vmem_limit_bytes=24 << 20),
        name="begin",
    )(coefs, mine)


def end(groups, plain, *rest):
    everything = plain.shape[1]
    return pl.pallas_call(
        end_kernel,
        out_shape=shape(2 * groups, STATES, 2, everything // groups // 2),
        in_specs=[in_vmem()] * 6,
        out_specs=in_vmem(),
        scratch_shapes=[pltpu.VMEM((1, everything), jnp.float32), pltpu.VMEM((ROWS, everything), jnp.float32)],
        compiler_params=pltpu.CompilerParams(vmem_limit_bytes=24 << 20),
        name="end",
    )(plain, *rest)


def call(kernel, shapes, *arrays):
    return pl.pallas_call(
        kernel,
        out_shape=shapes,
        in_specs=[in_vmem()] * len(arrays),
        out_specs=jax.tree.map(lambda _: in_vmem(), shapes),
        compiler_params=pltpu.CompilerParams(vmem_limit_bytes=4 << 20),
    )(*arrays)


def pack_kernel(atoms_ref, params_ref, own_ref):
    width = atoms_ref.shape[1]
    own_ref[0, :ATOM_ROWS] = atoms_ref[...]
    own_ref[0, ATOM_ROWS:ONE_ROW] = params_ref[...]
    own_ref[0, ONE_ROW : ONE_ROW + 1] = jnp.ones((1, width), jnp.float32)
    own_ref[0, ONE_ROW + 1 :] = jnp.zeros((ROWS - ONE_ROW - 1, width), jnp.float32)


def project_kernel(signals_ref, basis_ref, out_ref, signals, basis, sems):
    copies = [
        pltpu.make_async_copy(signals_ref, signals, sems.at[0]),
        pltpu.make_async_copy(basis_ref, basis, sems.at[1]),
    ]
    for copy in copies:
        copy.start()
    for copy in copies:
        copy.wait()
    sums = jnp.dot(basis[...], signals[...], preferred_element_type=jnp.float32)
    half = sums.shape[1] // 2
    rows = jnp.concatenate([sums[:, :half], sums[:, half:]], axis=0)
    for r in range(PACKED):
        block = rows[4 * r : 4 * r + 4]
        for i in range(out_ref.shape[0]):
            out_ref[i, r] = block


def project(signals, basis, slots):
    arrays = [pltpu.with_memory_space_constraint(array, pltpu.HBM) for array in (signals, basis)]
    return pl.pallas_call(
        project_kernel,
        out_shape=shape(slots, PACKED, 4, signals.shape[1] // 2),
        in_specs=[pl.BlockSpec(memory_space=pltpu.HBM)] * 2,
        out_specs=in_vmem(),
        scratch_shapes=[pltpu.VMEM(array.shape, array.dtype) for array in arrays] + [pltpu.SemaphoreType.DMA((2,))],
        compiler_params=pltpu.CompilerParams(vmem_limit_bytes=4 << 20),
        name="project",
    )(*arrays)


def add_kernel(parts_ref, out_ref):
    total = jnp.sum(parts_ref[...], axis=0)
    for i in range(out_ref.shape[0]):
        out_ref[i] = total


def merged(states):
    peak = jnp.max(states[:, 0], axis=0)
    factors = jnp.exp2(states[:, 0] - peak[None])
    return [peak] + [jnp.sum(states[:, i] * factors, axis=0) for i in range(1, STATES)]


def merge_kernel(states_ref, out_ref):
    state = merged(states_ref[...])
    for i in range(out_ref.shape[0]):
        for j in range(STATES):
            out_ref[i, j] = state[j]


def finish_kernel(states_ref, maps_ref):
    _, total, *weighted = merged(states_ref[...])
    half = total.shape[1]
    for j, value in enumerate(weighted):
        result = value / total
        for h in range(2):
            maps_ref[j : j + 1, h * half : (h + 1) * half] = result[h : h + 1]


def shape(*sizes):
    return jax.ShapeDtypeStruct(sizes, jnp.float32)


def exchange(array, axis, mask):
    return lax.ppermute(array, axis, [(i, i ^ mask) for i in range(lax.axis_size(axis))])


def along_x(array, first):
    count = lax.axis_size("x")
    order = [(i + first) % count for i in range(count)]
    return lax.all_to_all(array, "x", 0, 0, axis_index_groups=[order])


def along_z(array, first):
    count = lax.axis_size(("zh", "zl"))
    order = [(i + first) % count for i in range(count)]
    return lax.all_to_all(array, ("zh", "zl"), 0, 0, axis_index_groups=[order])


def on_device(signals, basis, atoms, params):
    width, half = atoms.shape[1], signals.shape[1] // 2
    across, along = lax.axis_size("x"), lax.axis_size(("zh", "zl"))
    sums = project(signals, basis, across)
    sums = along_x(sums, 3)
    own = call(pack_kernel, shape(1, ROWS, width), atoms, params)
    near = exchange(own, "y", 1)
    sums = call(add_kernel, shape(along, PACKED, 4, half), sums)
    coefs = along_z(sums, COEFS_FROM)
    pair = jnp.concatenate([own, near])
    core = exchange(pair, "c", 1)
    four = jnp.concatenate([pair, core])
    far = exchange(four, "y", 2)

    groups = along // 2
    plain, shifted, peak, sums, coefficients = begin(coefs, four)
    states = end(groups, plain, shifted, peak, sums, four, far)
    states = along_z(states, STATES_FROM)
    states = call(merge_kernel, shape(across, STATES, 2, half), states)
    states = along_x(states, 2)
    maps = call(finish_kernel, shape(3, 2 * half), states)
    return coefficients, maps


def solution(mesh):
    sizes = dict(zip(("x", "zh", "y", "zl", "c"), (4, 2, 4, 8, 2)))
    fine = Mesh(mesh.devices.reshape(tuple(sizes.values())), tuple(sizes))
    af, vert = ("x", "zh"), ("y", "zl", "c")
    return jax.shard_map(
        on_device,
        mesh=fine,
        in_specs=(P(af, vert), P(None, af), P(None, af + vert), P(None, af + vert)),
        out_specs=(P(None, vert), P(None, vert)),
        check_vma=False,
    )
```

```python
import math

import jax
import jax.numpy as jnp
from jax import lax
from jax.experimental import pallas as pl
from jax.experimental.pallas import tpu as pltpu
from jax.sharding import Mesh
from jax.sharding import PartitionSpec as P


scale = 1.5 * math.log2(math.e)
margin, limit = 80.0, 2.0**120

ATOM_ROWS, ONE_ROW, ROWS = 10, 13, 16
PACKED, STATES = 5, 5
COEFS_FROM, STATES_FROM = 10, 8
SAMPLE = 128
TILE = 1024


def split(values):
    high = values.astype(jnp.bfloat16)
    rest = values - high.astype(jnp.float32)
    middle = rest.astype(jnp.bfloat16)
    low = (rest - middle.astype(jnp.float32)).astype(jnp.bfloat16)
    return high, middle, low


def stack(values):
    high, middle, low = split(values)
    return jnp.concatenate([high, middle, low, high, middle, high], axis=0)


def atom_terms(piece):
    high, middle, low = split(piece)
    return jnp.concatenate([high, high, high, middle, middle, low], axis=0)


def row_index():
    return lax.broadcasted_iota(jnp.int32, (ROWS, 1), 0)


def param_terms(piece):
    row = row_index()
    kept = jnp.where((row >= ATOM_ROWS) & (row <= ONE_ROW), piece, 0.0)
    high, middle, low = split(kept)
    rolled = (
        high.astype(jnp.float32)
        + pltpu.roll(middle.astype(jnp.float32), 6, 0)
        + pltpu.roll(low.astype(jnp.float32), 10, 0)
    )
    return rolled.astype(jnp.bfloat16)


def scores_of(terms, stacked):
    return lax.dot_general(terms, stacked, (((0,), (0,)), ((), ())), preferred_element_type=jnp.float32)


def weigh(params, weights):
    high = weights.astype(jnp.bfloat16)
    low = (weights - high.astype(jnp.float32)).astype(jnp.bfloat16)
    twice, both = jnp.concatenate([params, params], axis=1), jnp.concatenate([high, low], axis=0)
    return jnp.dot(twice, both, preferred_element_type=jnp.float32)


def over_pieces(refs, step):
    for pieces in refs:
        count = pieces.shape[0]
        if count == 1:
            step(pieces, 0)
        else:
            lax.fori_loop(0, count, lambda i, _, pieces=pieces: (step(pieces, i), 0)[1], 0)


def add_weights(pieces, shifted, sums):
    everything, count = shifted.shape[1], pieces.shape[0]
    terms = [(atom_terms(pieces[i]), param_terms(pieces[i])) for i in range(count)]
    for at in range(0, everything, TILE):
        tile = slice(at, at + TILE)
        for i in range(0, count, 2):
            left, right = [], []
            for atoms, params in terms[i : i + 2]:
                weights = jnp.exp2(scores_of(atoms, shifted[:, tile]))
                high = weights.astype(jnp.bfloat16)
                left += [params, params]
                right += [high, (weights - high.astype(jnp.float32)).astype(jnp.bfloat16)]
            sums[:, tile] += jnp.dot(
                jnp.concatenate(left, axis=1), jnp.concatenate(right, axis=0), preferred_element_type=jnp.float32
            )


def begin_kernel(coefs_ref, near_ref, plain, shifted, peak, sums, own_coefs_ref, kept, sem):
    groups = coefs_ref.shape[0] // 2
    half = coefs_ref.shape[3]

    def rows_of(zl):
        at = (zl + 2 * groups - COEFS_FROM) % groups
        return jnp.concatenate([coefs_ref[at, r] + coefs_ref[groups + at, r] for r in range(PACKED)], axis=0)

    mine = rows_of(lax.axis_index("zl"))
    kept[:, :half] = mine[:ATOM_ROWS]
    kept[:, half:] = mine[ATOM_ROWS:]
    copy = pltpu.make_async_copy(kept, own_coefs_ref, sem)
    copy.start()

    zeros = jnp.zeros((ROWS - ATOM_ROWS, half), jnp.float32)
    for g in range(groups):
        both = scale * rows_of(g)
        for h in range(2):
            part = both[h * ATOM_ROWS : (h + 1) * ATOM_ROWS]
            at = (2 * g + h) * half
            plain[:, at : at + half] = jnp.concatenate([part, zeros], axis=0)

    sample = scores_of(atom_terms(near_ref[0])[:, :SAMPLE], stack(plain[...]))
    peak[...] = margin + jnp.max(sample, axis=0, keepdims=True)
    shifted[...] = stack(jnp.where(row_index() == ONE_ROW, -peak[...], plain[...]))
    sums[...] = jnp.zeros_like(sums)
    add_weights(near_ref, shifted, sums)
    copy.wait()


def end_kernel(plain, shifted, first_peak, first_sums, near_ref, far_ref, state_ref, peak, sums):
    groups = state_ref.shape[0] // 2
    half = state_ref.shape[3]
    peak[...] = first_peak[...]
    sums[...] = first_sums[...]
    add_weights(far_ref, shifted, sums)
    fine = jnp.all(sums[ONE_ROW : ONE_ROW + 1, :] < limit)

    @pl.when(jnp.logical_not(fine))
    def _():
        sums[...] = jnp.zeros_like(sums)

        def step(pieces, i):
            piece = pieces[i]
            scores = scores_of(atom_terms(piece), stack(plain[...]))
            top = jnp.maximum(peak[...], jnp.max(scores, axis=0, keepdims=True))
            sums[...] = sums[...] * jnp.exp2(peak[...] - top) + weigh(param_terms(piece), jnp.exp2(scores - top))
            peak[...] = top

        over_pieces((near_ref, far_ref), step)

    total = sums[ONE_ROW : ONE_ROW + 1, :]
    shift = jnp.round(jnp.log2(total))
    down = jnp.exp2(-shift)
    weighted = (sums[10:13, :] + sums[0:3, :] + sums[4:7, :]) * down
    values = (peak[...] + shift, total * down, weighted[0:1], weighted[1:2], weighted[2:3])
    for g in range(groups):
        for i, value in enumerate(values):
            for h in range(2):
                at = (2 * g + h) * half
                row = value[:, at : at + half]
                slot = (g - STATES_FROM) % groups
                state_ref[slot, i, h : h + 1] = row
                state_ref[groups + slot, i, h : h + 1] = row


def in_vmem():
    return pl.BlockSpec(memory_space=pltpu.VMEM)


def begin(coefs, mine):
    groups, voxels = coefs.shape[0] // 2, 2 * coefs.shape[3]
    everything = groups * voxels
    return pl.pallas_call(
        begin_kernel,
        out_shape=(
            shape(ROWS, everything),
            jax.ShapeDtypeStruct((6 * ROWS, everything), jnp.bfloat16),
            shape(1, everything),
            shape(ROWS, everything),
            shape(ATOM_ROWS, voxels),
        ),
        in_specs=[in_vmem()] * 2,
        out_specs=(in_vmem(),) * 4 + (pl.BlockSpec(memory_space=pl.ANY),),
        scratch_shapes=[pltpu.VMEM((ATOM_ROWS, voxels), jnp.float32), pltpu.SemaphoreType.DMA],
        compiler_params=pltpu.CompilerParams(vmem_limit_bytes=24 << 20),
        name="begin",
    )(coefs, mine)


def end(groups, plain, *rest):
    everything = plain.shape[1]
    return pl.pallas_call(
        end_kernel,
        out_shape=shape(2 * groups, STATES, 2, everything // groups // 2),
        in_specs=[in_vmem()] * 6,
        out_specs=in_vmem(),
        scratch_shapes=[pltpu.VMEM((1, everything), jnp.float32), pltpu.VMEM((ROWS, everything), jnp.float32)],
        compiler_params=pltpu.CompilerParams(vmem_limit_bytes=24 << 20),
        name="end",
    )(plain, *rest)


def call(kernel, shapes, *arrays):
    return pl.pallas_call(
        kernel,
        out_shape=shapes,
        in_specs=[in_vmem()] * len(arrays),
        out_specs=jax.tree.map(lambda _: in_vmem(), shapes),
        compiler_params=pltpu.CompilerParams(vmem_limit_bytes=4 << 20),
    )(*arrays)


def pack_kernel(atoms_ref, params_ref, own_ref):
    width = atoms_ref.shape[1]
    own_ref[0, :ATOM_ROWS] = atoms_ref[...]
    own_ref[0, ATOM_ROWS:ONE_ROW] = params_ref[...]
    own_ref[0, ONE_ROW : ONE_ROW + 1] = jnp.ones((1, width), jnp.float32)
    own_ref[0, ONE_ROW + 1 :] = jnp.zeros((ROWS - ONE_ROW - 1, width), jnp.float32)


def project_kernel(signals_ref, basis_ref, out_ref, signals, basis, sems):
    copies = [
        pltpu.make_async_copy(signals_ref, signals, sems.at[0]),
        pltpu.make_async_copy(basis_ref, basis, sems.at[1]),
    ]
    for copy in copies:
        copy.start()
    for copy in copies:
        copy.wait()
    sums = jnp.dot(basis[...], signals[...], preferred_element_type=jnp.float32)
    half = sums.shape[1] // 2
    rows = jnp.concatenate([sums[:, :half], sums[:, half:]], axis=0)
    for r in range(PACKED):
        block = rows[4 * r : 4 * r + 4]
        for i in range(out_ref.shape[0]):
            out_ref[i, r] = block


def project(signals, basis, slots):
    arrays = [pltpu.with_memory_space_constraint(array, pltpu.HBM) for array in (signals, basis)]
    return pl.pallas_call(
        project_kernel,
        out_shape=shape(slots, PACKED, 4, signals.shape[1] // 2),
        in_specs=[pl.BlockSpec(memory_space=pltpu.HBM)] * 2,
        out_specs=in_vmem(),
        scratch_shapes=[pltpu.VMEM(array.shape, array.dtype) for array in arrays] + [pltpu.SemaphoreType.DMA((2,))],
        compiler_params=pltpu.CompilerParams(vmem_limit_bytes=4 << 20),
        name="project",
    )(*arrays)


def add_kernel(parts_ref, out_ref):
    total = jnp.sum(parts_ref[...], axis=0)
    for i in range(out_ref.shape[0]):
        out_ref[i] = total


def merged(states):
    peak = jnp.max(states[:, 0], axis=0)
    factors = jnp.exp2(states[:, 0] - peak[None])
    return [peak] + [jnp.sum(states[:, i] * factors, axis=0) for i in range(1, STATES)]


def merge_kernel(states_ref, out_ref):
    state = merged(states_ref[...])
    for i in range(out_ref.shape[0]):
        for j in range(STATES):
            out_ref[i, j] = state[j]


def finish_kernel(states_ref, maps_ref):
    _, total, *weighted = merged(states_ref[...])
    half = total.shape[1]
    for j, value in enumerate(weighted):
        result = value / total
        for h in range(2):
            maps_ref[j : j + 1, h * half : (h + 1) * half] = result[h : h + 1]


def shape(*sizes):
    return jax.ShapeDtypeStruct(sizes, jnp.float32)


def exchange(array, axis, mask):
    return lax.ppermute(array, axis, [(i, i ^ mask) for i in range(lax.axis_size(axis))])


def along_x(array, first):
    count = lax.axis_size("x")
    order = [(i + first) % count for i in range(count)]
    return lax.all_to_all(array, "x", 0, 0, axis_index_groups=[order])


def along_z(array, first):
    count = lax.axis_size(("zh", "zl"))
    order = [(i + first) % count for i in range(count)]
    return lax.all_to_all(array, ("zh", "zl"), 0, 0, axis_index_groups=[order])


def on_device(signals, basis, atoms, params):
    width, half = atoms.shape[1], signals.shape[1] // 2
    across, along = lax.axis_size("x"), lax.axis_size(("zh", "zl"))
    sums = project(signals, basis, across)
    sums = along_x(sums, 3)
    own = call(pack_kernel, shape(1, ROWS, width), atoms, params)
    near = exchange(own, "y", 1)
    sums = call(add_kernel, shape(along, PACKED, 4, half), sums)
    coefs = along_z(sums, COEFS_FROM)
    pair = jnp.concatenate([own, near])
    core = exchange(pair, "c", 1)
    four = jnp.concatenate([pair, core])
    far = exchange(four, "y", 2)

    groups = along // 2
    plain, shifted, peak, sums, coefficients = begin(coefs, four)
    states = end(groups, plain, shifted, peak, sums, four, far)
    states = along_z(states, STATES_FROM)
    states = call(merge_kernel, shape(across, STATES, 2, half), states)
    states = along_x(states, 2)
    maps = call(finish_kernel, shape(3, 2 * half), states)
    return coefficients, maps


def solution(mesh):
    sizes = dict(zip(("x", "zh", "y", "zl", "c"), (4, 2, 4, 8, 2)))
    fine = Mesh(mesh.devices.reshape(tuple(sizes.values())), tuple(sizes))
    af, vert = ("x", "zh"), ("y", "zl", "c")
    return jax.shard_map(
        on_device,
        mesh=fine,
        in_specs=(P(af, vert), P(None, af), P(None, af + vert), P(None, af + vert)),
        out_specs=(P(None, vert), P(None, vert)),
        check_vma=False,
    )
```
